32 devices in a mesh: seq: 8 (over z, x), dp: 4 (over y, core).
Axes of the slice: x: 2, y: 2, z: 4, core: 2. Of those that a mesh axis runs over, the one named last changes fastest.
Arguments:
- queries: bfloat16 [8192, 4096], P(('dp', 'seq')), parts along dimension 0, may hold values from -6 to 6
- keys: bfloat16 [8192, 4096], P(('dp', 'seq')), parts along dimension 0, may hold values from -6 to 6
- values: bfloat16 [8192, 4096], P(('dp', 'seq')), parts along dimension 0, may hold values from -6 to 6
- gain: float32 [4096], replicated, may hold values from 0.1 to 1.9
- cotangent: bfloat16 [8192, 4096], P(('dp', 'seq')), parts along dimension 0, may hold values from -6 to 6
Outputs:
- key_grad: bfloat16 [8192, 4096], P(('dp', 'seq')), parts along dimension 0
- value_grad: bfloat16 [8192, 4096], P(('dp', 'seq')), parts along dimension 0
The draws below stay inside these ranges and needn't reach their ends.
There are 4 independent parts, one for each index of `dp`. The reference program is written for one: setup_inputs(seed, part) draws one part's arguments, and reference() takes and returns one part's arrays. A program takes and returns all parts, laid end to end along the dimension named above; an argument that names none is the same for every part. Nothing has to cross between parts.
All inputs are finite; a program needn't handle non-finite values.
Results may differ from the reference program's by a relative error of at most 0.0059.
Values may be sent and summed in bfloat16 or wider, within the bound.
No kernel may reach another device: no remote copies, remote signals or barrier semaphores. Data moves between devices by JAX's collectives and lax.ppermute only.
A program may use at most 64 MiB of HBM per device.

```python
from functools import partial
import jax
import jax.numpy as jnp
from jax import lax

HEADS = 32
DH = 128
TOK_DEV = 256
WIDTH = 4096
TOKENS = 2048
N_SEQ = 8


def levels(stream_key, shape, pieces, low, high):
    def one(axis_at, parts):
        draws = jax.random.uniform(jax.random.fold_in(jax.random.fold_in(stream_key, 6), axis_at), (parts,), jnp.float32, low / len(pieces), high / len(pieces))
        return jnp.repeat(jnp.exp(draws), shape[axis_at] // parts).reshape((-1,) + (1,) * (len(shape) - axis_at - 1))

    level = one(*pieces[0])
    for cut in pieces[1:]:
        level = level * one(*cut)
    return level


def noise(stream_key, extent, width, most, shards=(), kind=jnp.bfloat16):
    result = jax.random.normal(stream_key, extent, jnp.float32) * width
    if len(shards) > 0:
        result = levels(stream_key, extent, shards, -0.22, 0.18) * result
    return jnp.clip(result, min=-most, max=most).astype(kind)


def setup_inputs(seed: int = 0, part: int = 0) -> dict:
    key_of = jax.random.split(jax.random.key(seed), 6)
    part_keys = jax.random.split(jax.random.fold_in(key_of[5], part), 6)
    return {
        "queries": noise(part_keys[0], (TOKENS, WIDTH), 1.0, 6.0, ((0, 8),)),
        "keys": noise(part_keys[1], (TOKENS, WIDTH), 1.0, 6.0, ((0, 8),)),
        "values": noise(part_keys[2], (TOKENS, WIDTH), 1.0, 6.0, ((0, 8),)),
        "gain": jnp.clip(1.0 + 0.18 * jax.random.normal(key_of[3], (WIDTH,), jnp.float32), 0.1, 1.9),
        "cotangent": noise(part_keys[4], (TOKENS, WIDTH), 1.0, 6.0, ((0, 8),)),
    }


epsilon = 1e-05

def round_trip(tensor):
    return lax.optimization_barrier(tensor.astype(jnp.bfloat16)).astype(jnp.float32)

def rms_norm(attended, gain):
    mean_square = lax.optimization_barrier(jnp.mean(attended * attended, axis=-1, keepdims=True)) + epsilon
    return attended * lax.rsqrt(mean_square) * gain.astype(jnp.float32)

def reference(queries, keys, values, gain, cotangent):
    block_shape = (N_SEQ, TOK_DEV, HEADS, DH)
    query_heads = queries.reshape(block_shape).astype(jnp.float32)
    key_heads = keys.reshape(block_shape).astype(jnp.float32)
    value_heads = values.reshape(block_shape).astype(jnp.float32)
    states = jnp.einsum('nthd,nthe->nhde', key_heads, value_heads)
    running = jnp.cumsum(states, axis=0)
    prefix = jnp.concatenate([jnp.zeros_like(states[:1]), running[:-1]], axis=0)
    positions = jnp.arange(TOK_DEV)
    causal_mask = (positions[:, None] >= positions[None, :])[None]
    later_mask = (positions[:, None] <= positions[None, :])[None]

    def forward_block(block_items):
        query_block, key_block, value_block, prefix_block = block_items
        cross_term = jnp.einsum('thd,hde->the', query_block, round_trip(prefix_block))
        scores = jnp.einsum('thd,shd->hts', query_block, key_block)
        weights = round_trip(jnp.where(causal_mask, scores, 0.0))
        return cross_term + jnp.einsum('hts,she->the', weights, value_block)
    attended = lax.map(forward_block, (query_heads, key_heads, value_heads, prefix))
    attended = attended.reshape(TOKENS, HEADS * DH)
    _, pullback = jax.vjp(partial(rms_norm, gain=gain), attended)
    grad_out, = pullback(cotangent.astype(jnp.float32))
    grad_heads = round_trip(grad_out).reshape(block_shape)
    grad_states = jnp.einsum('nthd,nthe->nhde', query_heads, grad_heads)
    after = jnp.cumsum(grad_states[::-1], axis=0)[::-1]
    suffix = jnp.concatenate([after[1:], jnp.zeros_like(grad_states[:1])], axis=0)

    def backward_block(block_items):
        query_block, key_block, value_block, grad_block, suffix_block = block_items
        suffix_round = round_trip(suffix_block)
        value_scores = jnp.einsum('she,the->hst', value_block, grad_block)
        value_weights = round_trip(jnp.where(later_mask, value_scores, 0.0))
        key_out = jnp.einsum('hst,thd->shd', value_weights, query_block) + jnp.einsum('she,hde->shd', value_block, suffix_round)
        key_scores = jnp.einsum('shd,thd->hst', key_block, query_block)
        key_weights = round_trip(jnp.where(later_mask, key_scores, 0.0))
        value_out = jnp.einsum('hst,the->she', key_weights, grad_block) + jnp.einsum('shd,hde->she', key_block, suffix_round)
        return (key_out.astype(jnp.bfloat16), value_out.astype(jnp.bfloat16))
    key_grad, value_grad = lax.map(backward_block, (query_heads, key_heads, value_heads, grad_heads, suffix))
    return (key_grad.reshape(TOKENS, HEADS * DH), value_grad.reshape(TOKENS, HEADS * DH))
```

```python
from functools import partial

import jax
import jax.numpy as jnp
from jax import lax
from jax.experimental import pallas as pl
from jax.experimental.pallas import tpu as pltpu
from jax.sharding import PartitionSpec as P

DH = 128
EPS = 1e-05
CHUNKS = 2
F32 = jnp.float32
BF16 = jnp.bfloat16
NT = (((1,), (1,)), ((), ()))
NN = (((1,), (0,)), ((), ()))
TN = (((0,), (0,)), ((), ()))


def mm(a, b, dims):
    return lax.dot_general(a, b, dims, preferred_element_type=F32)


def head(h):
    return slice(h * DH, (h + 1) * DH)


def lower_mask(t):
    rows = lax.broadcasted_iota(jnp.int32, (t, t), 0)
    cols = lax.broadcasted_iota(jnp.int32, (t, t), 1)
    return rows >= cols


def state_kernel(heads, m_ref, a_ref, b_ref, *outs):
    step = pl.program_id(0)
    for j, out in enumerate(outs):
        @pl.when(step == j)
        def _():
            for h in range(heads):
                out[head(h), :] = mm(a_ref[:, head(h)], b_ref[:, head(h)], TN).astype(BF16)


def local_kernel(heads, q_ref, k_ref, v_ref, out_ref):
    mask = lower_mask(q_ref.shape[0])
    for h in range(heads):
        scores = mm(q_ref[:, head(h)], k_ref[:, head(h)], NT)
        weights = jnp.where(mask, scores, 0.0).astype(BF16)
        out_ref[:, head(h)] = mm(weights, v_ref[:, head(h)], NN)


def attend_kernel(heads, m_ref, q_ref, loc_ref, c_ref, gain_ref, *rest):
    count = len(rest) - 3
    prefixes, (att_ref, ss_ref, sc_ref) = rest[:count], rest[count:]
    step = pl.program_id(0)

    @pl.when(step == 0)
    def _():
        ss_ref[...] = jnp.zeros_like(ss_ref)
        sc_ref[...] = jnp.zeros_like(sc_ref)

    for j, pre in enumerate(prefixes):
        @pl.when(step == j)
        def _():
            ss = ss_ref[...]
            sc = sc_ref[...]
            for h in range(heads):
                att = loc_ref[:, head(h)] + mm(q_ref[:, head(h)], pre[head(h), :], NN)
                att_ref[:, head(h)] = att
                ss = ss + att * att
                sc = sc + att * (c_ref[:, head(h)].astype(F32) * gain_ref[:, head(h)])
            ss_ref[...] = ss
            sc_ref[...] = sc


def grad_kernel(heads, width, m_ref, q_ref, att_ref, c_ref, gain_ref, *rest):
    sums, rest = rest[: 2 * CHUNKS], rest[2 * CHUNKS :]
    g_ref, outs, (r_ref, s_ref) = rest[0], rest[1:-2], rest[-2:]
    step = pl.program_id(0)

    @pl.when(step == 0)
    def _():
        ss = sums[0][...]
        sc = sums[1][...]
        for i in range(1, CHUNKS):
            ss = ss + sums[2 * i][...]
            sc = sc + sums[2 * i + 1][...]
        ss = jnp.sum(ss, axis=1, keepdims=True) / width
        sc = jnp.sum(sc, axis=1, keepdims=True) / width
        r = lax.rsqrt(ss + EPS)
        r_ref[...] = jnp.broadcast_to(r, r_ref.shape)
        s_ref[...] = jnp.broadcast_to(r * r * r * sc, s_ref.shape)

    for j, out in enumerate(outs):
        @pl.when(step == j)
        def _():
            r = r_ref[...]
            s = s_ref[...]
            for h in range(heads):
                u = c_ref[:, head(h)].astype(F32) * gain_ref[:, head(h)]
                g = (u * r - att_ref[:, head(h)] * s).astype(BF16)
                g_ref[:, head(h)] = g
                out[head(h), :] = mm(q_ref[:, head(h)], g, TN).astype(BF16)


def back_local_kernel(heads, q_ref, k_ref, v_ref, g_ref, kl_ref, vl_ref):
    t = q_ref.shape[0]
    rows = lax.broadcasted_iota(jnp.int32, (t, t), 0)
    cols = lax.broadcasted_iota(jnp.int32, (t, t), 1)
    mask = rows <= cols
    for h in range(heads):
        q, k, v, g = (ref[:, head(h)] for ref in (q_ref, k_ref, v_ref, g_ref))
        vw = jnp.where(mask, mm(v, g, NT), 0.0).astype(BF16)
        kl_ref[:, head(h)] = mm(vw, q, NN)
        kw = jnp.where(mask, mm(k, q, NT), 0.0).astype(BF16)
        vl_ref[:, head(h)] = mm(kw, g, NN)


def finish_kernel(heads, count, m_ref, k_ref, v_ref, kl_ref, vl_ref, *rest):
    kg_ref, vg_ref = rest[-2:]
    step = pl.program_id(0)
    for j, suf in enumerate(rest[:count]):
        @pl.when(step == j)
        def _():
            for h in range(heads):
                s = suf[head(h), :]
                kg_ref[:, head(h)] = (kl_ref[:, head(h)] + mm(v_ref[:, head(h)], s, NT)).astype(BF16)
                vg_ref[:, head(h)] = (vl_ref[:, head(h)] + mm(k_ref[:, head(h)], s, NN)).astype(BF16)


def exchange(parts, n):
    m = len(parts)
    out = [parts[0]] + [None] * (m - 1)
    for j in range(m - 1, 0, -1):
        perm = [(i, (i // m) * m + ((i % m) ^ j)) for i in range(n)]
        out[j] = lax.ppermute(parts[j], "seq", perm)
    return out


def carry_groups(total, n, m, forward):
    groups = n // m

    def shift(x, by):
        step = by * m
        if forward:
            perm = [(i, i + step) for i in range(n - step)]
        else:
            perm = [(i + step, i) for i in range(n - step)]
        return lax.ppermute(x, "seq", perm)

    if groups == 1:
        return None
    if groups == 2:
        return shift(total.astype(BF16), 1).astype(F32)
    run = shift(total, 1)
    by = 1
    while by < groups - 1:
        run = run + shift(run, by)
        by *= 2
    return run


def spread(states, n, member, forward):
    m = len(states)
    got = exchange(states, n)
    got = [x.astype(F32) for x in got]
    carry = carry_groups(sum(got), n, m, forward)
    back = []
    for j in range(m):
        target = member ^ j
        acc = carry
        for i in range(m):
            source = member ^ i
            if i == j:
                continue
            take = (source < target) if forward else (source > target)
            term = jnp.where(take, got[i], 0.0)
            acc = term if acc is None else acc + term
        if acc is None:
            acc = jnp.zeros_like(got[0])
        back.append(acc.astype(BF16))
    return exchange(back, n)


def shards(n, queries, keys, values, gain, cotangent):
    rows, width = queries.shape
    m = 4 if n % 4 == 0 else (2 if n % 2 == 0 else 1)
    part = width // (CHUNKS * m)
    half = width // CHUNKS
    heads = part // DH
    member = lax.axis_index("seq") % m
    mem = member.reshape(1).astype(jnp.int32)
    gain2 = gain.reshape(1, width)
    stat = jax.ShapeDtypeStruct((rows, DH), F32)
    state = jax.ShapeDtypeStruct((part, DH), BF16)

    def cols(c, r=rows):
        return pl.BlockSpec((r, part), lambda j, s: (0, c * m + (s[0] ^ j)))

    def cols_half(r=rows):
        return pl.BlockSpec((r, part), lambda j, s: (0, s[0] ^ j))

    whole_state = pl.BlockSpec((part, DH), lambda j, s: (0, 0))
    whole_stat = pl.BlockSpec((rows, DH), lambda j, s: (0, 0))

    def call(kernel, args, in_specs, out_specs, out_shape, flops, nbytes, scratch=(), alias={}):
        return pl.pallas_call(
            kernel,
            out_shape=out_shape,
            grid_spec=pltpu.PrefetchScalarGridSpec(
                num_scalar_prefetch=1, grid=(m,), in_specs=in_specs, out_specs=out_specs, scratch_shapes=scratch
            ),
            input_output_aliases=alias,
            compiler_params=pltpu.CompilerParams(dimension_semantics=("arbitrary",), vmem_limit_bytes=24 << 20),
            cost_estimate=pl.CostEstimate(flops=flops, bytes_accessed=nbytes, transcendentals=0),
        )(mem, *args)

    unit = 2 * rows * DH * half

    def states_of(c, a, b):
        return call(partial(state_kernel, heads), (a, b), [cols(c), cols(c)], [whole_state] * m, [state] * m,
                    unit, 4 * rows * half + 2 * DH * half)

    plain = pl.BlockSpec((rows, part), lambda j: (0, j))

    def grid_call(kernel, args, outs, flops, nbytes):
        return pl.pallas_call(
            kernel,
            grid=(width // part,),
            in_specs=[plain] * len(args),
            out_specs=[plain] * outs,
            out_shape=[jax.ShapeDtypeStruct((rows, width), F32)] * outs,
            compiler_params=pltpu.CompilerParams(dimension_semantics=("arbitrary",), vmem_limit_bytes=24 << 20),
            cost_estimate=pl.CostEstimate(flops=flops, bytes_accessed=nbytes, transcendentals=0),
        )(*args)

    state_parts = [states_of(c, keys, values) for c in range(CHUNKS)]
    prefix = [spread(s, n, member, True) for s in state_parts]
    (local,) = grid_call(partial(local_kernel, heads), (queries, keys, values), 1, 8 * unit, 10 * rows * width)

    attended, sums = [], []
    for c in range(CHUNKS):
        att, ss, sc = call(
            partial(attend_kernel, heads),
            (queries, local, cotangent, gain2, *prefix[c]),
            [cols(c), cols(c), cols(c), cols(c, 1)] + [whole_state] * m,
            [cols_half(), whole_stat, whole_stat],
            [jax.ShapeDtypeStruct((rows, half), F32), stat, stat],
            unit, 12 * rows * half,
        )
        attended.append(att)
        sums += [ss, sc]

    grads, grad_parts = [], []
    for c in range(CHUNKS):
        g, *parts = call(
            partial(grad_kernel, heads, width),
            (queries, attended[c], cotangent, gain2, *sums),
            [cols(c), cols_half(), cols(c), cols(c, 1)] + [whole_stat] * (2 * CHUNKS),
            [cols_half()] + [whole_state] * m,
            [jax.ShapeDtypeStruct((rows, half), BF16)] + [state] * m,
            unit, 10 * rows * half,
            scratch=[pltpu.VMEM((rows, DH), F32)] * 2,
        )
        grads.append(g)
        grad_parts.append(parts)

    suffix = [spread(s, n, member, False) for s in grad_parts]
    blocks = half // part
    local_grads = []
    for c in range(CHUNKS):
        col = pl.BlockSpec((rows, part), lambda j, c=c: (0, c * blocks + j))
        own = pl.BlockSpec((rows, part), lambda j: (0, j))
        local_grads.append(pl.pallas_call(
            partial(back_local_kernel, heads),
            grid=(blocks,),
            in_specs=[col, col, col, own],
            out_specs=[own, own],
            out_shape=[jax.ShapeDtypeStruct((rows, half), F32)] * 2,
            compiler_params=pltpu.CompilerParams(dimension_semantics=("arbitrary",), vmem_limit_bytes=24 << 20),
            cost_estimate=pl.CostEstimate(flops=8 * unit, bytes_accessed=16 * rows * half, transcendentals=0),
        )(queries, keys, values, grads[c]))

    outs = ()
    out_shape = [jax.ShapeDtypeStruct((rows, width), BF16)] * 2
    for c in range(CHUNKS):
        base = 5 + m
        outs = call(
            partial(finish_kernel, heads, m),
            (keys, values, *local_grads[c], *suffix[c], *outs),
            [cols(c), cols(c), cols_half(), cols_half()] + [whole_state] * m
            + [pl.BlockSpec(memory_space=pl.ANY)] * len(outs),
            [cols(c), cols(c)],
            out_shape,
            2 * unit, 16 * rows * half,
            alias={base: 0, base + 1: 1} if outs else {},
        )
    return tuple(outs)


def solution(mesh):
    spec = P(("dp", "seq"), None)
    return jax.shard_map(
        partial(shards, mesh.shape["seq"]),
        mesh=mesh,
        in_specs=(spec, spec, spec, P(), spec),
        out_specs=(spec, spec),
        check_vma=False,
    )
```

```python
from functools import partial

import jax
import jax.numpy as jnp
from jax import lax
from jax.experimental import pallas as pl
from jax.experimental.pallas import tpu as pltpu
from jax.sharding import PartitionSpec as P

DH = 128
EPS = 1e-05
CHUNKS = 2
F32 = jnp.float32
BF16 = jnp.bfloat16
NT = (((1,), (1,)), ((), ()))
NN = (((1,), (0,)), ((), ()))
TN = (((0,), (0,)), ((), ()))


def mm(a, b, dims):
    return lax.dot_general(a, b, dims, preferred_element_type=F32)


def head(h):
    return slice(h * DH, (h + 1) * DH)


def lower_mask(t):
    rows = lax.broadcasted_iota(jnp.int32, (t, t), 0)
    cols = lax.broadcasted_iota(jnp.int32, (t, t), 1)
    return rows >= cols


def state_kernel(heads, m_ref, a_ref, b_ref, *outs):
    step = pl.program_id(0)
    for j, out in enumerate(outs):
        @pl.when(step == j)
        def _():
            for h in range(heads):
                out[head(h), :] = mm(a_ref[:, head(h)], b_ref[:, head(h)], TN).astype(BF16)


def local_kernel(heads, q_ref, k_ref, v_ref, out_ref):
    mask = lower_mask(q_ref.shape[0])
    for h in range(heads):
        scores = mm(q_ref[:, head(h)], k_ref[:, head(h)], NT)
        weights = jnp.where(mask, scores, 0.0).astype(BF16)
        out_ref[:, head(h)] = mm(weights, v_ref[:, head(h)], NN)


def attend_kernel(heads, m_ref, q_ref, loc_ref, c_ref, gain_ref, *rest):
    count = len(rest) - 3
    prefixes, (att_ref, ss_ref, sc_ref) = rest[:count], rest[count:]
    step = pl.program_id(0)

    @pl.when(step == 0)
    def _():
        ss_ref[...] = jnp.zeros_like(ss_ref)
        sc_ref[...] = jnp.zeros_like(sc_ref)

    for j, pre in enumerate(prefixes):
        @pl.when(step == j)
        def _():
            ss = ss_ref[...]
            sc = sc_ref[...]
            for h in range(heads):
                att = loc_ref[:, head(h)] + mm(q_ref[:, head(h)], pre[head(h), :], NN)
                att_ref[:, head(h)] = att
                ss = ss + att * att
                sc = sc + att * (c_ref[:, head(h)].astype(F32) * gain_ref[:, head(h)])
            ss_ref[...] = ss
            sc_ref[...] = sc


def grad_kernel(heads, width, m_ref, q_ref, att_ref, c_ref, gain_ref, *rest):
    sums, rest = rest[: 2 * CHUNKS], rest[2 * CHUNKS :]
    g_ref, outs, (r_ref, s_ref) = rest[0], rest[1:-2], rest[-2:]
    step = pl.program_id(0)

    @pl.when(step == 0)
    def _():
        ss = sums[0][...]
        sc = sums[1][...]
        for i in range(1, CHUNKS):
            ss = ss + sums[2 * i][...]
            sc = sc + sums[2 * i + 1][...]
        ss = jnp.sum(ss, axis=1, keepdims=True) / width
        sc = jnp.sum(sc, axis=1, keepdims=True) / width
        r = lax.rsqrt(ss + EPS)
        r_ref[...] = jnp.broadcast_to(r, r_ref.shape)
        s_ref[...] = jnp.broadcast_to(r * r * r * sc, s_ref.shape)

    for j, out in enumerate(outs):
        @pl.when(step == j)
        def _():
            r = r_ref[...]
            s = s_ref[...]
            for h in range(heads):
                u = c_ref[:, head(h)].astype(F32) * gain_ref[:, head(h)]
                g = (u * r - att_ref[:, head(h)] * s).astype(BF16)
                g_ref[:, head(h)] = g
                out[head(h), :] = mm(q_ref[:, head(h)], g, TN).astype(BF16)


def back_local_kernel(heads, q_ref, k_ref, v_ref, g_ref, kl_ref, vl_ref):
    t = q_ref.shape[0]
    rows = lax.broadcasted_iota(jnp.int32, (t, t), 0)
    cols = lax.broadcasted_iota(jnp.int32, (t, t), 1)
    mask = rows <= cols
    for h in range(heads):
        q, k, v, g = (ref[:, head(h)] for ref in (q_ref, k_ref, v_ref, g_ref))
        vw = jnp.where(mask, mm(v, g, NT), 0.0).astype(BF16)
        kl_ref[:, head(h)] = mm(vw, q, NN)
        kw = jnp.where(mask, mm(k, q, NT), 0.0).astype(BF16)
        vl_ref[:, head(h)] = mm(kw, g, NN)


def finish_kernel(heads, count, m_ref, k_ref, v_ref, kl_ref, vl_ref, *rest):
    kg_ref, vg_ref = rest[-2:]
    step = pl.program_id(0)
    for j, suf in enumerate(rest[:count]):
        @pl.when(step == j)
        def _():
            for h in range(heads):
                s = suf[head(h), :]
                kg_ref[:, head(h)] = (kl_ref[:, head(h)] + mm(v_ref[:, head(h)], s, NT)).astype(BF16)
                vg_ref[:, head(h)] = (vl_ref[:, head(h)] + mm(k_ref[:, head(h)], s, NN)).astype(BF16)


def exchange(parts, n):
    m = len(parts)
    out = [parts[0]] + [None] * (m - 1)
    for j in range(m - 1, 0, -1):
        perm = [(i, (i // m) * m + ((i % m) ^ j)) for i in range(n)]
        out[j] = lax.ppermute(parts[j], "seq", perm)
    return out


def carry_groups(total, n, m, forward):
    groups = n // m

    def shift(x, by):
        step = by * m
        if forward:
            perm = [(i, i + step) for i in range(n - step)]
        else:
            perm = [(i + step, i) for i in range(n - step)]
        return lax.ppermute(x, "seq", perm)

    if groups == 1:
        return None
    if groups == 2:
        return shift(total.astype(BF16), 1).astype(F32)
    run = shift(total, 1)
    by = 1
    while by < groups - 1:
        run = run + shift(run, by)
        by *= 2
    return run


def spread(states, n, member, forward, filler):
    m = len(states)
    got = exchange(states, n)
    got, first = lax.optimization_barrier((got, filler[0]))
    got = [x.astype(F32) for x in got]
    carry = carry_groups(sum(got), n, m, forward)
    carry, second = lax.optimization_barrier((carry, filler[1]))
    back = []
    for j in range(m):
        target = member ^ j
        acc = carry
        for i in range(m):
            source = member ^ i
            if i == j:
                continue
            take = (source < target) if forward else (source > target)
            term = jnp.where(take, got[i], 0.0)
            acc = term if acc is None else acc + term
        if acc is None:
            acc = jnp.zeros_like(got[0])
        back.append(acc.astype(BF16))
    return exchange(back, n), first, second


def shards(n, queries, keys, values, gain, cotangent):
    rows, width = queries.shape
    queries, keys, values, cotangent = (
        pltpu.with_memory_space_constraint(x, pltpu.HBM) for x in (queries, keys, values, cotangent)
    )
    m = 4 if n % 4 == 0 else (2 if n % 2 == 0 else 1)
    part = width // (CHUNKS * m)
    half = width // CHUNKS
    heads = part // DH
    member = lax.axis_index("seq") % m
    mem = member.reshape(1).astype(jnp.int32)
    gain2 = gain.reshape(1, width)
    stat = jax.ShapeDtypeStruct((rows, DH), F32)
    state = jax.ShapeDtypeStruct((part, DH), BF16)

    def cols(c, r=rows):
        return pl.BlockSpec((r, part), lambda j, s: (0, c * m + (s[0] ^ j)))

    def cols_half(r=rows):
        return pl.BlockSpec((r, part), lambda j, s: (0, s[0] ^ j))

    whole_state = pl.BlockSpec((part, DH), lambda j, s: (0, 0))
    whole_stat = pl.BlockSpec((rows, DH), lambda j, s: (0, 0))

    def call(kernel, args, in_specs, out_specs, out_shape, flops, nbytes, scratch=(), alias={}):
        return pl.pallas_call(
            kernel,
            out_shape=out_shape,
            grid_spec=pltpu.PrefetchScalarGridSpec(
                num_scalar_prefetch=1, grid=(m,), in_specs=in_specs, out_specs=out_specs, scratch_shapes=scratch
            ),
            input_output_aliases=alias,
            compiler_params=pltpu.CompilerParams(dimension_semantics=("arbitrary",), vmem_limit_bytes=24 << 20),
            cost_estimate=pl.CostEstimate(flops=flops, bytes_accessed=nbytes, transcendentals=0),
        )(mem, *args)

    unit = 2 * rows * DH * half

    def states_of(c, a, b):
        return call(partial(state_kernel, heads), (a, b), [cols(c), cols(c)], [whole_state] * m, [state] * m,
                    unit, 4 * rows * half + 2 * DH * half)

    state_parts = [states_of(c, keys, values) for c in range(CHUNKS)]

    def on_half(kernel, c, args, own_args, outs):
        col = pl.BlockSpec((rows, part), lambda j: (0, c * m + j))
        own = pl.BlockSpec((rows, part), lambda j: (0, j))
        return pl.pallas_call(
            partial(kernel, heads),
            grid=(m,),
            in_specs=[col] * len(args) + [own] * len(own_args),
            out_specs=[own] * outs,
            out_shape=[jax.ShapeDtypeStruct((rows, half), F32)] * outs,
            compiler_params=pltpu.CompilerParams(dimension_semantics=("arbitrary",), vmem_limit_bytes=24 << 20),
            cost_estimate=pl.CostEstimate(
                flops=4 * unit * outs, bytes_accessed=8 * rows * half * outs, transcendentals=0
            ),
        )(*args, *own_args)

    local = [on_half(local_kernel, c, (queries, keys, values), (), 1) for c in range(CHUNKS)]
    prefix = []
    for c in range(CHUNKS):
        filler = ((local[0], []), ([], local[1]))[c]
        pre, first, second = spread(state_parts[c], n, member, True, filler)
        local[c] = (first, second)[c]
        prefix.append(pre)

    attended, sums = [], []
    for c in range(CHUNKS):
        att, ss, sc = call(
            partial(attend_kernel, heads),
            (queries, *local[c], cotangent, gain2, *prefix[c]),
            [cols(c), cols_half(), cols(c), cols(c, 1)] + [whole_state] * m,
            [cols_half(), whole_stat, whole_stat],
            [jax.ShapeDtypeStruct((rows, half), F32), stat, stat],
            unit, 12 * rows * half,
        )
        attended.append(att)
        sums += [ss, sc]

    grads, grad_parts = [], []
    for c in range(CHUNKS):
        g, *parts = call(
            partial(grad_kernel, heads, width),
            (queries, attended[c], cotangent, gain2, *sums),
            [cols(c), cols_half(), cols(c), cols(c, 1)] + [whole_stat] * (2 * CHUNKS),
            [cols_half()] + [whole_state] * m,
            [jax.ShapeDtypeStruct((rows, half), BF16)] + [state] * m,
            unit, 10 * rows * half,
            scratch=[pltpu.VMEM((rows, DH), F32)] * 2,
        )
        grads.append(g)
        grad_parts.append(parts)

    local_grads = [on_half(back_local_kernel, c, (queries, keys, values), (grads[c],), 2) for c in range(CHUNKS)]
    suffix = []
    for c in range(CHUNKS):
        filler = ((local_grads[0], []), ([], local_grads[1]))[c]
        suf, first, second = spread(grad_parts[c], n, member, False, filler)
        local_grads[c] = (first, second)[c]
        suffix.append(suf)

    outs = ()
    out_shape = [jax.ShapeDtypeStruct((rows, width), BF16)] * 2
    for c in range(CHUNKS):
        base = 5 + m
        outs = call(
            partial(finish_kernel, heads, m),
            (keys, values, *local_grads[c], *suffix[c], *outs),
            [cols(c), cols(c), cols_half(), cols_half()] + [whole_state] * m
            + [pl.BlockSpec(memory_space=pl.ANY)] * len(outs),
            [cols(c), cols(c)],
            out_shape,
            2 * unit, 16 * rows * half,
            alias={base: 0, base + 1: 1} if outs else {},
        )
    return tuple(outs)


def solution(mesh):
    spec = P(("dp", "seq"), None)
    return jax.shard_map(
        partial(shards, mesh.shape["seq"]),
        mesh=mesh,
        in_specs=(spec, spec, spec, P(), spec),
        out_specs=(spec, spec),
        check_vma=False,
    )
```

```python
from functools import partial

import jax
import jax.numpy as jnp
from jax import lax
from jax.experimental import pallas as pl
from jax.experimental.pallas import tpu as pltpu
from jax.sharding import PartitionSpec as P

DH = 128
EPS = 1e-05
CHUNKS = 2
F32 = jnp.float32
BF16 = jnp.bfloat16
NT = (((1,), (1,)), ((), ()))
NN = (((1,), (0,)), ((), ()))
TN = (((0,), (0,)), ((), ()))
VMEM = pl.BlockSpec(memory_space=pltpu.VMEM)
SMEM = pl.BlockSpec(memory_space=pltpu.SMEM)
HBM = pl.BlockSpec(memory_space=pltpu.HBM)
barrier = lax.optimization_barrier


def mm(a, b, dims):
    return lax.dot_general(a, b, dims, preferred_element_type=F32)


def head(h):
    return slice(h * DH, (h + 1) * DH)


def head_at(offset, h):
    return pl.ds(pl.multiple_of(offset + h * DH, DH), DH)


def owned(member, j, part):
    return pl.multiple_of((member ^ j) * part, part)


def mask_of(t, later):
    rows = lax.broadcasted_iota(jnp.int32, (t, t), 0)
    cols = lax.broadcasted_iota(jnp.int32, (t, t), 1)
    return rows <= cols if later else rows >= cols


def state_kernel(chunk, part, m, mem, k_hbm, v_hbm, k_ref, v_ref, *rest):
    outs, sem = rest[:m], rest[m]
    member = mem[0]
    copies = []
    for j in reversed(range(m)):
        at = owned(member, j, part)
        far = pl.multiple_of(chunk * m * part + at, part)
        pair = []
        for i, (src, dst) in enumerate(((k_hbm, k_ref), (v_hbm, v_ref))):
            copy = pltpu.make_async_copy(src.at[:, pl.ds(far, part)], dst.at[:, pl.ds(at, part)], sem.at[i, j])
            copy.start()
            pair.append(copy)
        copies.append((j, at, pair))
    for j, at, pair in copies:
        for copy in pair:
            copy.wait()
        for h in range(part // DH):
            a, b = k_ref[:, head_at(at, h)], v_ref[:, head_at(at, h)]
            outs[j][head(h), :] = mm(a, b, TN).astype(BF16)


def local_kernel(chunk, part, m, k_ref, v_ref, gain_ref, q_hbm, c_hbm, q_ref, u_ref, loc_ref, c_ref, sem):
    copies = []
    for j in range(m):
        at, far = pl.ds(j * part, part), pl.ds((chunk * m + j) * part, part)
        pair = []
        for i, (src, dst) in enumerate(((q_hbm, q_ref), (c_hbm, c_ref))):
            copy = pltpu.make_async_copy(src.at[:, far], dst.at[:, at], sem.at[i, j])
            copy.start()
            pair.append(copy)
        copies.append(pair)
    mask = mask_of(q_ref.shape[0], False)
    for j, pair in enumerate(copies):
        for copy in pair:
            copy.wait()
        for h in range(j * part // DH, (j + 1) * part // DH):
            scores = mm(q_ref[:, head(h)], k_ref[:, head(h)], NT)
            weights = jnp.where(mask, scores, 0.0).astype(BF16)
            loc_ref[:, head(h)] = mm(weights, v_ref[:, head(h)], NN)
            here = head(chunk * m * part // DH + h)
            u_ref[:, head(h)] = c_ref[:, head(h)].astype(F32) * gain_ref[:, here]


def attend_kernel(part, m, mem, q_ref, loc_ref, u_ref, *rest):
    prefixes, (att_ref, ss_ref, su_ref) = rest[:m], rest[m:]
    member = mem[0]
    ss = jnp.zeros(ss_ref.shape, F32)
    su = jnp.zeros(su_ref.shape, F32)
    for j in range(m):
        at = owned(member, j, part)
        for h in range(part // DH):
            here = head_at(at, h)
            att = loc_ref[:, here] + mm(q_ref[:, here], prefixes[j][head(h), :], NN)
            att_ref[:, here] = att
            ss = ss + att * att
            su = su + att * u_ref[:, here]
    ss_ref[...] = ss
    su_ref[...] = su


def grad_kernel(part, m, width, mem, q_ref, att_ref, u_ref, *rest):
    sums, rest = rest[: 2 * CHUNKS], rest[2 * CHUNKS :]
    g_ref, outs = rest[0], rest[1:]
    member = mem[0]
    ss = sums[0][...]
    su = sums[1][...]
    for i in range(1, CHUNKS):
        ss = ss + sums[2 * i][...]
        su = su + sums[2 * i + 1][...]
    ss = jnp.sum(ss, axis=1, keepdims=True) / width
    su = jnp.sum(su, axis=1, keepdims=True) / width
    r = lax.rsqrt(ss + EPS)
    s = jnp.broadcast_to(r * r * r * su, sums[0].shape)
    r = jnp.broadcast_to(r, sums[0].shape)
    for j in reversed(range(m)):
        at = owned(member, j, part)
        for h in range(part // DH):
            here = head_at(at, h)
            g = (u_ref[:, here] * r - att_ref[:, here] * s).astype(BF16)
            g_ref[:, here] = g
            outs[j][head(h), :] = mm(q_ref[:, here], g, TN).astype(BF16)


def back_local_kernel(q_ref, k_ref, v_ref, g_ref, kl_ref, vl_ref):
    mask = mask_of(q_ref.shape[0], True)
    for h in range(q_ref.shape[1] // DH):
        q, k, v, g = (ref[:, head(h)] for ref in (q_ref, k_ref, v_ref, g_ref))
        vw = jnp.where(mask, mm(v, g, NT), 0.0).astype(BF16)
        kl_ref[:, head(h)] = mm(vw, q, NN)
        kw = jnp.where(mask, mm(k, q, NT), 0.0).astype(BF16)
        vl_ref[:, head(h)] = mm(kw, g, NN)


def finish_kernel(chunk, part, m, mem, k_ref, v_ref, kl_ref, vl_ref, *rest):
    suffixes = rest[:m]
    kg_hbm, vg_hbm, kg_ref, vg_ref, sem = rest[-5:]
    member = mem[0]
    copies = []
    for j in range(m):
        at = owned(member, j, part)
        far = pl.multiple_of(chunk * m * part + at, part)
        for h in range(part // DH):
            here = head_at(at, h)
            s = suffixes[j][head(h), :]
            kg_ref[:, here] = (kl_ref[:, here] + mm(v_ref[:, here], s, NT)).astype(BF16)
            vg_ref[:, here] = (vl_ref[:, here] + mm(k_ref[:, here], s, NN)).astype(BF16)
        for i, (src, dst) in enumerate(((kg_ref, kg_hbm), (vg_ref, vg_hbm))):
            copy = pltpu.make_async_copy(src.at[:, pl.ds(at, part)], dst.at[:, pl.ds(far, part)], sem.at[i, j])
            copy.start()
            copies.append(copy)
    for copy in copies:
        copy.wait()


def exchange(parts, n):
    m = len(parts)
    out = [parts[0]] + [None] * (m - 1)
    for j in range(m - 1, 0, -1):
        perm = [(i, (i // m) * m + ((i % m) ^ j)) for i in range(n)]
        out[j] = lax.ppermute(parts[j], "seq", perm)
    return out


def carry_groups(total, n, m, forward):
    groups = n // m

    def shift(x, by):
        step = by * m
        if forward:
            perm = [(i, i + step) for i in range(n - step)]
        else:
            perm = [(i + step, i) for i in range(n - step)]
        return lax.ppermute(x, "seq", perm)

    if groups == 1:
        return jnp.zeros_like(total)
    if groups == 2:
        return shift(total.astype(BF16), 1)
    run = shift(total, 1)
    by = 1
    while by < groups - 1:
        run = run + shift(run, by)
        by *= 2
    return run


def give_back(got, carry, member, forward):
    back = []
    for j in range(len(got)):
        acc = carry.astype(F32)
        for i in range(len(got)):
            if i != j:
                source, target = member ^ i, member ^ j
                take = (source < target) if forward else (source > target)
                acc = acc + jnp.where(take, got[i].astype(F32), 0.0)
        back.append(acc.astype(BF16))
    return back


def total_of(got):
    return sum(x.astype(F32) for x in got)


def scan_chunks(first, second_of, n, member, forward, fill_a, fill_b):
    m = len(first)
    got_a = exchange(first, n)
    second, extra = second_of()
    got_a, second, extra = barrier((got_a, second, extra))
    carry_a = carry_groups(total_of(got_a), n, m, forward)
    got_b = exchange(second, n)
    made_a = fill_a(extra)
    carry_a, made_a, extra = barrier((carry_a, made_a, extra))
    back_a = exchange(give_back(got_a, carry_a, member, forward), n)
    carry_b = carry_groups(total_of(got_b), n, m, forward)
    made_b = fill_b(extra)
    carry_b, made_b = barrier((carry_b, made_b))
    back_b = exchange(give_back(got_b, carry_b, member, forward), n)
    return (back_a, back_b), (made_a, made_b)


def shards(n, queries, keys, values, gain, cotangent):
    rows, width = queries.shape
    queries, keys, values, cotangent = (
        pltpu.with_memory_space_constraint(x, pltpu.HBM) for x in (queries, keys, values, cotangent)
    )
    m = 4 if n % 4 == 0 else (2 if n % 2 == 0 else 1)
    half = width // CHUNKS
    part = half // m
    member = lax.axis_index("seq") % m
    mem = member.reshape(1).astype(jnp.int32)
    gain2 = gain.reshape(1, width)
    wide = pltpu.VMEM((rows, half), F32)
    slim = pltpu.VMEM((rows, half), BF16)
    stat = pltpu.VMEM((rows, DH), F32)
    state = pltpu.VMEM((part, DH), BF16)
    sems = pltpu.SemaphoreType.DMA((2, m))
    unit = 2 * rows * DH * half

    def call(kernel, args, in_specs, out_shape, flops, nbytes, scratch=(), out_specs=None, alias={}):
        return pl.pallas_call(
            kernel,
            in_specs=in_specs,
            out_specs=out_specs or [VMEM] * len(out_shape),
            out_shape=out_shape,
            scratch_shapes=scratch,
            input_output_aliases=alias,
            compiler_params=pltpu.CompilerParams(vmem_limit_bytes=12 << 20),
            cost_estimate=pl.CostEstimate(flops=flops, bytes_accessed=nbytes, transcendentals=0),
        )(*args)

    def states_of(c):
        k, v, *parts = call(
            partial(state_kernel, c, part, m), (mem, keys, values), [SMEM, HBM, HBM],
            [slim, slim] + [state] * m, unit, 6 * rows * half, [sems],
        )
        return parts, (k, v)

    def local_of(c, kv):
        return call(
            partial(local_kernel, c, part, m), (*kv, gain2, queries, cotangent), [VMEM, VMEM, VMEM, HBM, HBM],
            [slim, wide, wide], 4 * unit, 12 * rows * half, [slim, sems],
        )

    kv = [None, None]
    parts_a, kv[0] = states_of(0)

    def second_states():
        parts_b, kv_b = states_of(1)
        return parts_b, (kv[0], kv_b)

    def fill_a(extra):
        kv[0] = extra[0]
        return local_of(0, extra[0])

    def fill_b(extra):
        kv[1] = extra[1]
        return local_of(1, extra[1])

    prefix, made = scan_chunks(parts_a, second_states, n, member, True, fill_a, fill_b)

    attended, sums = [], []
    for c in range(CHUNKS):
        q, u, loc = made[c]
        att, ss, su = call(
            partial(attend_kernel, part, m), (mem, q, loc, u, *prefix[c]), [SMEM] + [VMEM] * (3 + m),
            [wide, stat, stat], unit, 4 * rows * half, alias={2: 0},
        )
        attended.append(att)
        sums += [ss, su]

    def grads_of(c):
        q, u, _ = made[c]
        g, *parts = call(
            partial(grad_kernel, part, m, width), (mem, q, attended[c], u, *sums),
            [SMEM] + [VMEM] * (3 + 2 * CHUNKS), [slim] + [state] * m, unit, 4 * rows * half,
        )
        return parts, (q, *kv[c], g)

    def back_local_of(qkvg):
        return call(back_local_kernel, qkvg, [VMEM] * 4, [wide, wide], 8 * unit, 8 * rows * half)

    parts_a, near_a = grads_of(0)

    def second_grads():
        parts_b, near_b = grads_of(1)
        return parts_b, (near_a, near_b)

    suffix, made = scan_chunks(
        parts_a, second_grads, n, member, False, lambda e: back_local_of(e[0]), lambda e: back_local_of(e[1])
    )

    outs = ()
    for c in range(CHUNKS):
        base = 5 + m
        outs = call(
            partial(finish_kernel, c, part, m), (mem, *kv[c], *made[c], *suffix[c], *outs),
            [SMEM] + [VMEM] * (4 + m) + [HBM] * len(outs),
            [jax.ShapeDtypeStruct((rows, width), BF16)] * 2, 2 * unit, 8 * rows * half, [slim, slim, sems],
            out_specs=[HBM, HBM], alias={base: 0, base + 1: 1} if outs else {},
        )
    return tuple(outs)


def solution(mesh):
    spec = P(("dp", "seq"), None)
    return jax.shard_map(
        partial(shards, mesh.shape["seq"]),
        mesh=mesh,
        in_specs=(spec, spec, spec, P(), spec),
        out_specs=(spec, spec),
        check_vma=False,
    )
```

```python
from functools import partial

import jax
import jax.numpy as jnp
from jax import lax
from jax.experimental import pallas as pl
from jax.experimental.pallas import tpu as pltpu
from jax.sharding import PartitionSpec as P

DH = 128
EPS = 1e-05
CHUNKS = 2
F32 = jnp.float32
BF16 = jnp.bfloat16
NT = (((1,), (1,)), ((), ()))
NN = (((1,), (0,)), ((), ()))
TN = (((0,), (0,)), ((), ()))
VMEM = pl.BlockSpec(memory_space=pltpu.VMEM)
SMEM = pl.BlockSpec(memory_space=pltpu.SMEM)
HBM = pl.BlockSpec(memory_space=pltpu.HBM)
barrier = lax.optimization_barrier


def mm(a, b, dims):
    return lax.dot_general(a, b, dims, preferred_element_type=F32)


def head(h):
    return slice(h * DH, (h + 1) * DH)


def head_at(offset, h):
    return pl.ds(pl.multiple_of(offset + h * DH, DH), DH)


def owned(member, j, part):
    return pl.multiple_of((member ^ j) * part, part)


def mask_of(t, later):
    rows = lax.broadcasted_iota(jnp.int32, (t, t), 0)
    cols = lax.broadcasted_iota(jnp.int32, (t, t), 1)
    return rows <= cols if later else rows >= cols


def state_kernel(chunk, part, m, mem, k_hbm, v_hbm, k_ref, v_ref, *rest):
    outs, sem = rest[:m], rest[m]
    member = mem[0]
    copies = []
    for j in reversed(range(m)):
        at = owned(member, j, part)
        far = pl.multiple_of(chunk * m * part + at, part)
        pair = []
        for i, (src, dst) in enumerate(((k_hbm, k_ref), (v_hbm, v_ref))):
            copy = pltpu.make_async_copy(src.at[:, pl.ds(far, part)], dst.at[:, pl.ds(at, part)], sem.at[i, j])
            copy.start()
            pair.append(copy)
        copies.append((j, at, pair))
    for j, at, pair in copies:
        for copy in pair:
            copy.wait()
        for h in range(part // DH):
            a, b = k_ref[:, head_at(at, h)], v_ref[:, head_at(at, h)]
            outs[j][head(h), :] = mm(a, b, TN).astype(BF16)


def local_kernel(chunk, part, m, k_ref, v_ref, gain_ref, q_hbm, c_hbm, q_ref, u_ref, loc_ref, c_ref, sem):
    copies = []
    for j in range(m):
        at, far = pl.ds(j * part, part), pl.ds((chunk * m + j) * part, part)
        pair = []
        for i, (src, dst) in enumerate(((q_hbm, q_ref), (c_hbm, c_ref))):
            copy = pltpu.make_async_copy(src.at[:, far], dst.at[:, at], sem.at[i, j])
            copy.start()
            pair.append(copy)
        copies.append(pair)
    mask = mask_of(q_ref.shape[0], False)
    for j, pair in enumerate(copies):
        for copy in pair:
            copy.wait()
        for h in range(j * part // DH, (j + 1) * part // DH):
            scores = mm(q_ref[:, head(h)], k_ref[:, head(h)], NT)
            weights = jnp.where(mask, scores, 0.0).astype(BF16)
            loc_ref[:, head(h)] = mm(weights, v_ref[:, head(h)], NN)
            here = head(chunk * m * part // DH + h)
            u_ref[:, head(h)] = c_ref[:, head(h)].astype(F32) * gain_ref[:, here]


def attend_kernel(part, m, mem, q_ref, loc_ref, u_ref, *rest):
    prefixes, (att_ref, ss_ref, su_ref) = rest[:m], rest[m:]
    member = mem[0]
    ss = jnp.zeros(ss_ref.shape, F32)
    su = jnp.zeros(su_ref.shape, F32)
    for j in range(m):
        at = owned(member, j, part)
        for h in range(part // DH):
            here = head_at(at, h)
            att = loc_ref[:, here] + mm(q_ref[:, here], prefixes[j][head(h), :], NN)
            att_ref[:, here] = att
            ss = ss + att * att
            su = su + att * u_ref[:, here]
    ss_ref[...] = ss
    su_ref[...] = su


def grad_kernel(part, m, width, mem, q_ref, att_ref, u_ref, *rest):
    sums, rest = rest[: 2 * CHUNKS], rest[2 * CHUNKS :]
    g_ref, outs = rest[0], rest[1:]
    member = mem[0]
    ss = sums[0][...]
    su = sums[1][...]
    for i in range(1, CHUNKS):
        ss = ss + sums[2 * i][...]
        su = su + sums[2 * i + 1][...]
    ss = jnp.sum(ss, axis=1, keepdims=True) / width
    su = jnp.sum(su, axis=1, keepdims=True) / width
    r = lax.rsqrt(ss + EPS)
    s = jnp.broadcast_to(r * r * r * su, sums[0].shape)
    r = jnp.broadcast_to(r, sums[0].shape)
    for j in reversed(range(m)):
        at = owned(member, j, part)
        for h in range(part // DH):
            here = head_at(at, h)
            g = (u_ref[:, here] * r - att_ref[:, here] * s).astype(BF16)
            g_ref[:, here] = g
            outs[j][head(h), :] = mm(q_ref[:, here], g, TN).astype(BF16)


def back_local_kernel(q_ref, k_ref, v_ref, g_ref, kl_ref, vl_ref):
    mask = mask_of(q_ref.shape[0], True)
    for h in range(q_ref.shape[1] // DH):
        q, k, v, g = (ref[:, head(h)] for ref in (q_ref, k_ref, v_ref, g_ref))
        vw = jnp.where(mask, mm(v, g, NT), 0.0).astype(BF16)
        kl_ref[:, head(h)] = mm(vw, q, NN)
        kw = jnp.where(mask, mm(k, q, NT), 0.0).astype(BF16)
        vl_ref[:, head(h)] = mm(kw, g, NN)


def finish_kernel(chunk, part, m, mem, k_ref, v_ref, kl_ref, vl_ref, *rest):
    suffixes = rest[:m]
    kg_hbm, vg_hbm, kg_ref, vg_ref, sem = rest[-5:]
    member = mem[0]
    copies = []
    for j in range(m):
        at = owned(member, j, part)
        far = pl.multiple_of(chunk * m * part + at, part)
        for h in range(part // DH):
            here = head_at(at, h)
            s = suffixes[j][head(h), :]
            kg_ref[:, here] = (kl_ref[:, here] + mm(v_ref[:, here], s, NT)).astype(BF16)
            vg_ref[:, here] = (vl_ref[:, here] + mm(k_ref[:, here], s, NN)).astype(BF16)
        for i, (src, dst) in enumerate(((kg_ref, kg_hbm), (vg_ref, vg_hbm))):
            copy = pltpu.make_async_copy(src.at[:, pl.ds(at, part)], dst.at[:, pl.ds(far, part)], sem.at[i, j])
            copy.start()
            copies.append(copy)
    for copy in copies:
        copy.wait()


def total_kernel(*refs):
    acc = refs[0][...].astype(F32)
    for ref in refs[1:-1]:
        acc = acc + ref[...].astype(F32)
    refs[-1][...] = acc.astype(refs[-1].dtype)


def give_back_kernel(m, forward, mem, carry, *refs):
    got, back = refs[:m], refs[m:]
    member = mem[0]
    for j in range(m):
        acc = carry[...].astype(F32)
        for i in range(m):
            if i != j:
                source, target = member ^ i, member ^ j
                take = (source < target) if forward else (source > target)
                acc = acc + jnp.where(take, got[i][...].astype(F32), 0.0)
        back[j][...] = acc.astype(BF16)


def call(kernel, args, in_specs, out_shape, flops, nbytes, scratch=(), out_specs=None, alias={}):
    return pl.pallas_call(
        kernel,
        in_specs=in_specs,
        out_specs=out_specs or [VMEM] * len(out_shape),
        out_shape=out_shape,
        scratch_shapes=scratch,
        input_output_aliases=alias,
        compiler_params=pltpu.CompilerParams(vmem_limit_bytes=8 << 20),
        cost_estimate=pl.CostEstimate(flops=flops, bytes_accessed=nbytes, transcendentals=0),
    )(*args)


def total_of(got, n):
    m = len(got)
    wire = BF16 if n // m == 2 else F32
    (total,) = call(total_kernel, got, [VMEM] * m, [pltpu.VMEM(got[0].shape, wire)], got[0].size, got[0].size)
    return total


def give_back(got, carry, mem, forward):
    m = len(got)
    return call(
        partial(give_back_kernel, m, forward), (mem, carry, *got), [SMEM] + [VMEM] * (m + 1),
        [pltpu.VMEM(got[0].shape, BF16)] * m, got[0].size, got[0].size,
    )


def exchange(parts, n):
    m = len(parts)
    out = [parts[0]] + [None] * (m - 1)
    for j in range(m - 1, 0, -1):
        perm = [(i, (i // m) * m + ((i % m) ^ j)) for i in range(n)]
        out[j] = lax.ppermute(parts[j], "seq", perm)
    return out


def carry_groups(total, n, m, forward):
    groups = n // m

    def shift(x, by):
        step = by * m
        if forward:
            perm = [(i, i + step) for i in range(n - step)]
        else:
            perm = [(i + step, i) for i in range(n - step)]
        return lax.ppermute(x, "seq", perm)

    if groups == 1:
        return jnp.zeros_like(total)
    if groups == 2:
        return shift(total, 1)
    run = shift(total, 1)
    by = 1
    while by < groups - 1:
        run = run + shift(run, by)
        by *= 2
    return run


def scan_chunks(first, second_of, n, mem, forward, fill_a, fill_b):
    m = len(first)
    got_a = exchange(first, n)
    second, extra = second_of()
    got_a, second, extra = barrier((got_a, second, extra))
    carry_a = carry_groups(total_of(got_a, n), n, m, forward)
    got_b = exchange(second, n)
    made_a = fill_a(extra)
    carry_a, made_a, extra = barrier((carry_a, made_a, extra))
    back_a = exchange(give_back(got_a, carry_a, mem, forward), n)
    carry_b = carry_groups(total_of(got_b, n), n, m, forward)
    made_b = fill_b(extra)
    carry_b, made_b = barrier((carry_b, made_b))
    back_b = exchange(give_back(got_b, carry_b, mem, forward), n)
    return (back_a, back_b), (made_a, made_b)


def shards(n, queries, keys, values, gain, cotangent):
    rows, width = queries.shape
    queries, keys, values, cotangent = (
        pltpu.with_memory_space_constraint(x, pltpu.HBM) for x in (queries, keys, values, cotangent)
    )
    m = 4 if n % 4 == 0 else (2 if n % 2 == 0 else 1)
    half = width // CHUNKS
    part = half // m
    member = lax.axis_index("seq") % m
    mem = member.reshape(1).astype(jnp.int32)
    gain2 = gain.reshape(1, width)
    wide = pltpu.VMEM((rows, half), F32)
    slim = pltpu.VMEM((rows, half), BF16)
    stat = pltpu.VMEM((rows, DH), F32)
    state = pltpu.VMEM((part, DH), BF16)
    sems = pltpu.SemaphoreType.DMA((2, m))
    unit = 2 * rows * DH * half

    def states_of(c):
        k, v, *parts = call(
            partial(state_kernel, c, part, m), (mem, keys, values), [SMEM, HBM, HBM],
            [slim, slim] + [state] * m, unit, 6 * rows * half, [sems],
        )
        return parts, (k, v)

    def local_of(c, kv):
        return call(
            partial(local_kernel, c, part, m), (*kv, gain2, queries, cotangent), [VMEM, VMEM, VMEM, HBM, HBM],
            [slim, wide, wide], 4 * unit, 12 * rows * half, [slim, sems],
        )

    kv = [None, None]
    parts_a, kv[0] = states_of(0)

    def second_states():
        parts_b, kv_b = states_of(1)
        return parts_b, (kv[0], kv_b)

    def fill_a(extra):
        kv[0] = extra[0]
        return local_of(0, extra[0])

    def fill_b(extra):
        kv[1] = extra[1]
        return local_of(1, extra[1])

    prefix, made = scan_chunks(parts_a, second_states, n, mem, True, fill_a, fill_b)

    attended, sums = [], []
    for c in range(CHUNKS):
        q, u, loc = made[c]
        att, ss, su = call(
            partial(attend_kernel, part, m), (mem, q, loc, u, *prefix[c]), [SMEM] + [VMEM] * (3 + m),
            [wide, stat, stat], unit, 4 * rows * half, alias={2: 0},
        )
        attended.append(att)
        sums += [ss, su]

    def grads_of(c):
        q, u, _ = made[c]
        g, *parts = call(
            partial(grad_kernel, part, m, width), (mem, q, attended[c], u, *sums),
            [SMEM] + [VMEM] * (3 + 2 * CHUNKS), [slim] + [state] * m, unit, 4 * rows * half,
        )
        return parts, (q, *kv[c], g)

    def back_local_of(qkvg):
        return call(back_local_kernel, qkvg, [VMEM] * 4, [wide, wide], 8 * unit, 8 * rows * half)

    parts_a, near_a = grads_of(0)

    def second_grads():
        parts_b, near_b = grads_of(1)
        return parts_b, (near_a, near_b)

    suffix, made = scan_chunks(
        parts_a, second_grads, n, mem, False, lambda e: back_local_of(e[0]), lambda e: back_local_of(e[1])
    )

    outs = ()
    for c in range(CHUNKS):
        base = 5 + m
        outs = call(
            partial(finish_kernel, c, part, m), (mem, *kv[c], *made[c], *suffix[c], *outs),
            [SMEM] + [VMEM] * (4 + m) + [HBM] * len(outs),
            [jax.ShapeDtypeStruct((rows, width), BF16)] * 2, 2 * unit, 8 * rows * half, [slim, slim, sems],
            out_specs=[HBM, HBM], alias={base: 0, base + 1: 1} if outs else {},
        )
    return tuple(outs)


def solution(mesh):
    spec = P(("dp", "seq"), None)
    return jax.shard_map(
        partial(shards, mesh.shape["seq"]),
        mesh=mesh,
        in_specs=(spec, spec, spec, P(), spec),
        out_specs=(spec, spec),
        check_vma=False,
    )
```

```python
from functools import partial

import jax
import jax.numpy as jnp
from jax import lax
from jax.experimental import pallas as pl
from jax.experimental.pallas import tpu as pltpu
from jax.sharding import PartitionSpec as P

DH = 128
EPS = 1e-05
CHUNKS = 2
F32 = jnp.float32
BF16 = jnp.bfloat16
NT = (((1,), (1,)), ((), ()))
NN = (((1,), (0,)), ((), ()))
TN = (((0,), (0,)), ((), ()))
VMEM = pl.BlockSpec(memory_space=pltpu.VMEM)
SMEM = pl.BlockSpec(memory_space=pltpu.SMEM)
HBM = pl.BlockSpec(memory_space=pltpu.HBM)
barrier = lax.optimization_barrier


def mm(a, b, dims):
    return lax.dot_general(a, b, dims, preferred_element_type=F32)


def head(h):
    return slice(h * DH, (h + 1) * DH)


def head_at(offset, h):
    return pl.ds(pl.multiple_of(offset + h * DH, DH), DH)


def owned(member, j, part):
    return pl.multiple_of((member ^ j) * part, part)


def mask_of(t, later):
    rows = lax.broadcasted_iota(jnp.int32, (t, t), 0)
    cols = lax.broadcasted_iota(jnp.int32, (t, t), 1)
    return rows <= cols if later else rows >= cols


def state_kernel(chunk, part, m, mem, k_hbm, v_hbm, k_ref, v_ref, *rest):
    outs, sem = rest[:m], rest[m]
    member = mem[0]
    copies = []
    for j in reversed(range(m)):
        at = owned(member, j, part)
        far = pl.multiple_of(chunk * m * part + at, part)
        pair = []
        for i, (src, dst) in enumerate(((k_hbm, k_ref), (v_hbm, v_ref))):
            copy = pltpu.make_async_copy(src.at[:, pl.ds(far, part)], dst.at[:, pl.ds(at, part)], sem.at[i, j])
            copy.start()
            pair.append(copy)
        copies.append((j, at, pair))
    for j, at, pair in copies:
        for copy in pair:
            copy.wait()
        for h in range(part // DH):
            a, b = k_ref[:, head_at(at, h)], v_ref[:, head_at(at, h)]
            outs[j][head(h), :] = mm(a, b, TN).astype(BF16)


def local_kernel(chunk, part, m, k_ref, v_ref, gain_ref, q_hbm, c_hbm, q_ref, u_ref, loc_ref, c_ref, sem):
    copies = []
    for j in range(m):
        at, far = pl.ds(j * part, part), pl.ds((chunk * m + j) * part, part)
        pair = []
        for i, (src, dst) in enumerate(((q_hbm, q_ref), (c_hbm, c_ref))):
            copy = pltpu.make_async_copy(src.at[:, far], dst.at[:, at], sem.at[i, j])
            copy.start()
            pair.append(copy)
        copies.append(pair)
    mask = mask_of(q_ref.shape[0], False)
    for j, pair in enumerate(copies):
        for copy in pair:
            copy.wait()
        for h in range(j * part // DH, (j + 1) * part // DH):
            scores = mm(q_ref[:, head(h)], k_ref[:, head(h)], NT)
            weights = jnp.where(mask, scores, 0.0).astype(BF16)
            loc_ref[:, head(h)] = mm(weights, v_ref[:, head(h)], NN)
            here = head(chunk * m * part // DH + h)
            u_ref[:, head(h)] = c_ref[:, head(h)].astype(F32) * gain_ref[:, here]


def attend_kernel(part, m, mem, q_ref, loc_ref, u_ref, *rest):
    prefixes, (att_ref, ss_ref, su_ref) = rest[:m], rest[m:]
    member = mem[0]
    ss = jnp.zeros(ss_ref.shape, F32)
    su = jnp.zeros(su_ref.shape, F32)
    for j in range(m):
        at = owned(member, j, part)
        for h in range(part // DH):
            here = head_at(at, h)
            att = loc_ref[:, here] + mm(q_ref[:, here], prefixes[j][head(h), :], NN)
            att_ref[:, here] = att
            ss = ss + att * att
            su = su + att * u_ref[:, here]
    ss_ref[...] = ss
    su_ref[...] = su


def grad_kernel(part, m, width, mem, q_ref, att_ref, u_ref, *rest):
    sums, rest = rest[: 2 * CHUNKS], rest[2 * CHUNKS :]
    g_ref, outs = rest[0], rest[1:]
    member = mem[0]
    ss = sums[0][...]
    su = sums[1][...]
    for i in range(1, CHUNKS):
        ss = ss + sums[2 * i][...]
        su = su + sums[2 * i + 1][...]
    ss = jnp.sum(ss, axis=1, keepdims=True) / width
    su = jnp.sum(su, axis=1, keepdims=True) / width
    r = lax.rsqrt(ss + EPS)
    s = jnp.broadcast_to(r * r * r * su, sums[0].shape)
    r = jnp.broadcast_to(r, sums[0].shape)
    for j in reversed(range(m)):
        at = owned(member, j, part)
        for h in range(part // DH):
            here = head_at(at, h)
            g = (u_ref[:, here] * r - att_ref[:, here] * s).astype(BF16)
            g_ref[:, here] = g
            outs[j][head(h), :] = mm(q_ref[:, here], g, TN).astype(BF16)


def back_local_kernel(q_ref, k_ref, v_ref, g_ref, kl_ref, vl_ref):
    mask = mask_of(q_ref.shape[0], True)
    for h in range(q_ref.shape[1] // DH):
        q, k, v, g = (ref[:, head(h)] for ref in (q_ref, k_ref, v_ref, g_ref))
        vw = jnp.where(mask, mm(v, g, NT), 0.0).astype(BF16)
        kl_ref[:, head(h)] = mm(vw, q, NN)
        kw = jnp.where(mask, mm(k, q, NT), 0.0).astype(BF16)
        vl_ref[:, head(h)] = mm(kw, g, NN)


def finish_kernel(chunk, part, m, mem, k_ref, v_ref, kl_ref, vl_ref, *rest):
    suffixes = rest[:m]
    kg_hbm, vg_hbm, kg_ref, vg_ref, sem = rest[-5:]
    member = mem[0]
    copies = []
    for j in range(m):
        at = owned(member, j, part)
        far = pl.multiple_of(chunk * m * part + at, part)
        for h in range(part // DH):
            here = head_at(at, h)
            s = suffixes[j][head(h), :]
            kg_ref[:, here] = (kl_ref[:, here] + mm(v_ref[:, here], s, NT)).astype(BF16)
            vg_ref[:, here] = (vl_ref[:, here] + mm(k_ref[:, here], s, NN)).astype(BF16)
        for i, (src, dst) in enumerate(((kg_ref, kg_hbm), (vg_ref, vg_hbm))):
            copy = pltpu.make_async_copy(src.at[:, pl.ds(at, part)], dst.at[:, pl.ds(far, part)], sem.at[i, j])
            copy.start()
            copies.append(copy)
    for copy in copies:
        copy.wait()


def total_kernel(*refs):
    acc = refs[0][...].astype(F32)
    for ref in refs[1:-1]:
        acc = acc + ref[...].astype(F32)
    refs[-1][...] = acc.astype(refs[-1].dtype)


def give_back_kernel(m, forward, mem, carry, *refs):
    got, back = refs[:m], refs[m:]
    member = mem[0]
    for j in range(m):
        acc = carry[...].astype(F32)
        for i in range(m):
            if i != j:
                source, target = member ^ i, member ^ j
                take = (source < target) if forward else (source > target)
                acc = acc + jnp.where(take, got[i][...].astype(F32), 0.0)
        back[j][...] = acc.astype(BF16)


def call(kernel, args, in_specs, out_shape, flops, nbytes, scratch=(), out_specs=None, alias={}):
    return pl.pallas_call(
        kernel,
        in_specs=in_specs,
        out_specs=out_specs or [VMEM] * len(out_shape),
        out_shape=out_shape,
        scratch_shapes=scratch,
        input_output_aliases=alias,
        compiler_params=pltpu.CompilerParams(vmem_limit_bytes=8 << 20),
        cost_estimate=pl.CostEstimate(flops=flops, bytes_accessed=nbytes, transcendentals=0),
    )(*args)


def total_of(got, n):
    m = len(got)
    wire = BF16 if n // m == 2 else F32
    (total,) = call(total_kernel, got, [VMEM] * m, [pltpu.VMEM(got[0].shape, wire)], got[0].size, got[0].size)
    return total


def give_back(got, carry, mem, forward):
    m = len(got)
    return call(
        partial(give_back_kernel, m, forward), (mem, carry, *got), [SMEM] + [VMEM] * (m + 1),
        [pltpu.VMEM(got[0].shape, BF16)] * m, got[0].size, got[0].size,
    )


def exchange(parts, n):
    m = len(parts)
    out = [parts[0]] + [None] * (m - 1)
    for j in range(m - 1, 0, -1):
        perm = [(i, (i // m) * m + ((i % m) ^ j)) for i in range(n)]
        out[j] = lax.ppermute(parts[j], "seq", perm)
    return out


def carry_groups(total, n, m, forward):
    groups = n // m

    def shift(x, by):
        step = by * m
        if forward:
            perm = [(i, i + step) for i in range(n - step)]
        else:
            perm = [(i + step, i) for i in range(n - step)]
        return lax.ppermute(x, "seq", perm)

    if groups == 1:
        return jnp.zeros_like(total)
    if groups == 2:
        return shift(total, 1)
    run = shift(total, 1)
    by = 1
    while by < groups - 1:
        run = run + shift(run, by)
        by *= 2
    return run


def scan_chunks(first, second_of, n, mem, forward, fill_a, fill_b):
    m = len(first)
    got_a = exchange(first, n)
    second, extra = second_of()
    got_b = exchange(second, n)
    made_a = fill_a(extra)
    got_b, made_a, extra = barrier((got_b, made_a, extra))
    carry_a = carry_groups(total_of(got_a, n), n, m, forward)
    carry_b = carry_groups(total_of(got_b, n), n, m, forward)
    made_b = fill_b(extra)
    carry_a, made_b = barrier((carry_a, made_b))
    back_a = exchange(give_back(got_a, carry_a, mem, forward), n)
    back_b = exchange(give_back(got_b, carry_b, mem, forward), n)
    return (back_a, back_b), (made_a, made_b)


def shards(n, queries, keys, values, gain, cotangent):
    rows, width = queries.shape
    queries, keys, values, cotangent = (
        pltpu.with_memory_space_constraint(x, pltpu.HBM) for x in (queries, keys, values, cotangent)
    )
    m = 4 if n % 4 == 0 else (2 if n % 2 == 0 else 1)
    half = width // CHUNKS
    part = half // m
    member = lax.axis_index("seq") % m
    mem = member.reshape(1).astype(jnp.int32)
    gain2 = gain.reshape(1, width)
    wide = pltpu.VMEM((rows, half), F32)
    slim = pltpu.VMEM((rows, half), BF16)
    stat = pltpu.VMEM((rows, DH), F32)
    state = pltpu.VMEM((part, DH), BF16)
    sems = pltpu.SemaphoreType.DMA((2, m))
    unit = 2 * rows * DH * half

    def states_of(c):
        k, v, *parts = call(
            partial(state_kernel, c, part, m), (mem, keys, values), [SMEM, HBM, HBM],
            [slim, slim] + [state] * m, unit, 6 * rows * half, [sems],
        )
        return parts, (k, v)

    def local_of(c, kv):
        return call(
            partial(local_kernel, c, part, m), (*kv, gain2, queries, cotangent), [VMEM, VMEM, VMEM, HBM, HBM],
            [slim, wide, wide], 4 * unit, 12 * rows * half, [slim, sems],
        )

    kv = [None, None]
    parts_a, kv[0] = states_of(0)

    def second_states():
        parts_b, kv_b = states_of(1)
        return parts_b, (kv[0], kv_b)

    def fill_a(extra):
        kv[0] = extra[0]
        return local_of(0, extra[0])

    def fill_b(extra):
        kv[1] = extra[1]
        return local_of(1, extra[1])

    prefix, made = scan_chunks(parts_a, second_states, n, mem, True, fill_a, fill_b)

    attended, sums = [], []
    for c in range(CHUNKS):
        q, u, loc = made[c]
        att, ss, su = call(
            partial(attend_kernel, part, m), (mem, q, loc, u, *prefix[c]), [SMEM] + [VMEM] * (3 + m),
            [wide, stat, stat], unit, 4 * rows * half, alias={2: 0},
        )
        attended.append(att)
        sums += [ss, su]

    def grads_of(c):
        q, u, _ = made[c]
        g, *parts = call(
            partial(grad_kernel, part, m, width), (mem, q, attended[c], u, *sums),
            [SMEM] + [VMEM] * (3 + 2 * CHUNKS), [slim] + [state] * m, unit, 4 * rows * half,
        )
        return parts, (q, *kv[c], g)

    def back_local_of(qkvg):
        return call(back_local_kernel, qkvg, [VMEM] * 4, [wide, wide], 8 * unit, 8 * rows * half)

    parts_a, near_a = grads_of(0)

    def second_grads():
        parts_b, near_b = grads_of(1)
        return parts_b, (near_a, near_b)

    suffix, made = scan_chunks(
        parts_a, second_grads, n, mem, False, lambda e: back_local_of(e[0]), lambda e: back_local_of(e[1])
    )

    outs = ()
    for c in range(CHUNKS):
        base = 5 + m
        outs = call(
            partial(finish_kernel, c, part, m), (mem, *kv[c], *made[c], *suffix[c], *outs),
            [SMEM] + [VMEM] * (4 + m) + [HBM] * len(outs),
            [jax.ShapeDtypeStruct((rows, width), BF16)] * 2, 2 * unit, 8 * rows * half, [slim, slim, sems],
            out_specs=[HBM, HBM], alias={base: 0, base + 1: 1} if outs else {},
        )
    return tuple(outs)


def solution(mesh):
    spec = P(("dp", "seq"), None)
    return jax.shard_map(
        partial(shards, mesh.shape["seq"]),
        mesh=mesh,
        in_specs=(spec, spec, spec, P(), spec),
        out_specs=(spec, spec),
        check_vma=False,
    )
```

```python
from functools import partial

import jax
import jax.numpy as jnp
from jax import lax
from jax.experimental import pallas as pl
from jax.experimental.pallas import tpu as pltpu
from jax.sharding import PartitionSpec as P

DH = 128
EPS = 1e-05
CHUNKS = 2
F32 = jnp.float32
BF16 = jnp.bfloat16
NT = (((1,), (1,)), ((), ()))
NN = (((1,), (0,)), ((), ()))
TN = (((0,), (0,)), ((), ()))
VMEM = pl.BlockSpec(memory_space=pltpu.VMEM)
HBM = pl.BlockSpec(memory_space=pltpu.HBM)
barrier = lax.optimization_barrier


def mm(a, b, dims):
    return lax.dot_general(a, b, dims, preferred_element_type=F32)


def head(h):
    return slice(h * DH, (h + 1) * DH)


def head_at(offset, h):
    return pl.ds(pl.multiple_of(offset + h * DH, DH), DH)


def owned(member, j, part):
    return pl.multiple_of((member ^ j) * part, part)


def mask_of(t, later):
    rows = lax.broadcasted_iota(jnp.int32, (t, t), 0)
    cols = lax.broadcasted_iota(jnp.int32, (t, t), 1)
    return rows <= cols if later else rows >= cols


def first_state_kernel(part, m, which, k_hbm, v_hbm, *rest):
    outs, (k_ref, v_ref, sem) = rest[:-3], rest[-3:]
    member = lax.rem(lax.axis_index("seq"), m)
    copies = []
    for j in which:
        at = owned(member, j, part)
        pair = []
        for i, (src, dst) in enumerate(((k_hbm, k_ref), (v_hbm, v_ref))):
            here = pl.ds(at, part)
            copy = pltpu.make_async_copy(src.at[:, here], dst.at[:, here], sem.at[i, j])
            copy.start()
            pair.append(copy)
        copies.append((j, at, pair))
    for out, (j, at, pair) in zip(outs, copies):
        for copy in pair:
            copy.wait()
        for h in range(part // DH):
            a, b = k_ref[:, head_at(at, h)], v_ref[:, head_at(at, h)]
            out[head(h), :] = mm(a, b, TN).astype(BF16)


def state_kernel(chunk, part, m, k_ref, v_ref, *outs):
    member = lax.rem(lax.axis_index("seq"), m)
    for j in reversed(range(m)):
        far = pl.multiple_of(chunk * m * part + owned(member, j, part), part)
        for h in range(part // DH):
            a, b = k_ref[:, head_at(far, h)], v_ref[:, head_at(far, h)]
            outs[j][head(h), :] = mm(a, b, TN).astype(BF16)


def local_kernel(first, q_ref, k_ref, v_ref, c_ref, gain_ref, u_ref, loc_ref):
    mask = mask_of(q_ref.shape[0], False)
    for h in range(u_ref.shape[1] // DH):
        far = head(first + h)
        scores = mm(q_ref[:, far], k_ref[:, far], NT)
        weights = jnp.where(mask, scores, 0.0).astype(BF16)
        loc_ref[:, head(h)] = mm(weights, v_ref[:, far], NN)
        u_ref[:, head(h)] = c_ref[:, far].astype(F32) * gain_ref[:, far]


def attend_kernel(chunk, part, m, which, width, q_ref, loc_ref, u_ref, *rest):
    count = len(which)
    prefixes, before, (att_ref, ss_ref, su_ref) = rest[:count], rest[count:-3], rest[-3:]
    member = lax.rem(lax.axis_index("seq"), m)
    if before:
        ss, su = before[0][...], before[1][...]
    else:
        ss = jnp.zeros(ss_ref.shape, F32)
        su = jnp.zeros(su_ref.shape, F32)
    for pre, j in zip(prefixes, which):
        at = owned(member, j, part)
        for h in range(part // DH):
            here = head_at(at, h)
            far = head_at(chunk * m * part + at, h)
            att = loc_ref[:, here] + mm(q_ref[:, far], pre[head(h), :], NN)
            att_ref[:, here] = att
            ss = ss + att * att
            su = su + att * u_ref[:, here]
    if width:
        r = lax.rsqrt(jnp.sum(ss, axis=1, keepdims=True) / width + EPS)
        su = r * r * r * (jnp.sum(su, axis=1, keepdims=True) / width)
        ss = r
    ss_ref[...] = jnp.broadcast_to(ss, ss_ref.shape)
    su_ref[...] = jnp.broadcast_to(su, su_ref.shape)


def grad_kernel(chunk, part, m, which, q_ref, att_ref, u_ref, r_ref, s_ref, *rest):
    g_ref, outs = rest[-len(which) - 1], rest[-len(which) :]
    member = lax.rem(lax.axis_index("seq"), m)
    r = r_ref[...]
    s = s_ref[...]
    for out, j in zip(outs, which):
        at = owned(member, j, part)
        for h in range(part // DH):
            here = head_at(at, h)
            g = (u_ref[:, here] * r - att_ref[:, here] * s).astype(BF16)
            g_ref[:, here] = g
            far = head_at(chunk * m * part + at, h)
            out[head(h), :] = mm(q_ref[:, far], g, TN).astype(BF16)


def back_local_kernel(first, q_ref, k_ref, v_ref, g_ref, kl_ref, vl_ref):
    mask = mask_of(q_ref.shape[0], True)
    for h in range(g_ref.shape[1] // DH):
        q, k, v = (ref[:, head(first + h)] for ref in (q_ref, k_ref, v_ref))
        g = g_ref[:, head(h)]
        vw = jnp.where(mask, mm(v, g, NT), 0.0).astype(BF16)
        kl_ref[:, head(h)] = mm(vw, q, NN)
        kw = jnp.where(mask, mm(k, q, NT), 0.0).astype(BF16)
        vl_ref[:, head(h)] = mm(kw, g, NN)


def finish_kernel(chunk, part, m, which, k_ref, v_ref, kl_ref, vl_ref, *rest):
    suffixes = rest[: len(which)]
    kg_hbm, vg_hbm, kg_ref, vg_ref, sem = rest[-5:]
    member = lax.rem(lax.axis_index("seq"), m)
    copies = []
    for suf, j in zip(suffixes, which):
        at = owned(member, j, part)
        far = pl.multiple_of(chunk * m * part + at, part)
        for h in range(part // DH):
            here = head_at(at, h)
            s = suf[head(h), :]
            own = head_at(far, h)
            kg_ref[:, here] = (kl_ref[:, here] + mm(v_ref[:, own], s, NT)).astype(BF16)
            vg_ref[:, here] = (vl_ref[:, here] + mm(k_ref[:, own], s, NN)).astype(BF16)
        for i, (src, dst) in enumerate(((kg_ref, kg_hbm), (vg_ref, vg_hbm))):
            copy = pltpu.make_async_copy(src.at[:, pl.ds(at, part)], dst.at[:, pl.ds(far, part)], sem.at[i, j])
            copy.start()
            copies.append(copy)
    for copy in copies:
        copy.wait()


def total_kernel(*refs):
    acc = refs[0][...].astype(F32)
    for ref in refs[1:-1]:
        acc = acc + ref[...].astype(F32)
    refs[-1][...] = acc.astype(refs[-1].dtype)


def give_back_kernel(m, forward, groups, carry, *refs):
    group = lax.axis_index("seq") // m
    use = group > 0 if forward else group < groups - 1
    got, back = refs[:m], refs[m:]
    member = lax.rem(lax.axis_index("seq"), m)
    for j in range(m):
        acc = jnp.where(use, carry[...].astype(F32), 0.0)
        for i in range(m):
            if i != j:
                source, target = member ^ i, member ^ j
                take = (source < target) if forward else (source > target)
                acc = acc + jnp.where(take, got[i][...].astype(F32), 0.0)
        back[j][...] = acc.astype(BF16)


def call(kernel, args, in_specs, out_shape, flops, nbytes, scratch=(), out_specs=None, alias={}):
    return pl.pallas_call(
        kernel,
        in_specs=in_specs,
        out_specs=out_specs or [VMEM] * len(out_shape),
        out_shape=out_shape,
        scratch_shapes=scratch,
        input_output_aliases=alias,
        compiler_params=pltpu.CompilerParams(vmem_limit_bytes=8 << 20),
        cost_estimate=pl.CostEstimate(flops=flops, bytes_accessed=nbytes, transcendentals=0),
    )(*args)


def total_of(got, n):
    m = len(got)
    wire = BF16 if n // m == 2 else F32
    (total,) = call(total_kernel, got, [VMEM] * m, [pltpu.VMEM(got[0].shape, wire)], got[0].size, got[0].size)
    return total


def give_back(got, carry, n, forward):
    m = len(got)
    return call(
        partial(give_back_kernel, m, forward, n // m), (carry, *got), [VMEM] * (m + 1),
        [pltpu.VMEM(got[0].shape, BF16)] * m, got[0].size, got[0].size,
    )


def exchange(parts, n):
    m = len(parts)
    out = [parts[0]] + [None] * (m - 1)
    for j in range(m - 1, 0, -1):
        perm = [(i, (i // m) * m + ((i % m) ^ j)) for i in range(n)]
        out[j] = lax.ppermute(parts[j], "seq", perm)
    return out


def carry_groups(total, n, m, forward):
    groups = n // m
    group = lax.axis_index("seq") // m

    def shift(x, by):
        step = by * m if forward else n - by * m
        return lax.ppermute(x, "seq", [(i, (i + step) % n) for i in range(n)])

    def shift_in(x, by):
        inside = group >= by if forward else group < groups - by
        return jnp.where(inside, shift(x, by), 0.0)

    if groups == 1:
        return total
    if groups == 2:
        return shift(total, 1)
    run = shift_in(total, 1)
    by = 1
    while by < groups - 1:
        run = run + shift_in(run, by)
        by *= 2
    return run


def scan_chunks(first, second_of, n, forward, fill_a, fill_b):
    m = len(first)
    got_a = exchange(first, n)
    second, extra = second_of()
    got_b = exchange(second, n)
    made_a = fill_a(extra)
    made_b = fill_b(extra)
    if forward:
        got_b, made_a, made_b = barrier((got_b, made_a, made_b))
    else:
        got_a, made_a = barrier((got_a, made_a))
    carry_a = carry_groups(total_of(got_a, n), n, m, forward)
    carry_b = carry_groups(total_of(got_b, n), n, m, forward)
    back_a = exchange(give_back(got_a, carry_a, n, forward), n)
    back_b = exchange(give_back(got_b, carry_b, n, forward), n)
    return (back_a, back_b), (made_a, made_b)


def shards(n, queries, keys, values, gain, cotangent):
    rows, width = queries.shape
    m = 4 if n % 4 == 0 else (2 if n % 2 == 0 else 1)
    half = width // CHUNKS
    part = half // m
    gain2 = gain.reshape(1, width)
    wide = pltpu.VMEM((rows, half), F32)
    slim = pltpu.VMEM((rows, half), BF16)
    stat = pltpu.VMEM((rows, DH), F32)
    state = pltpu.VMEM((part, DH), BF16)
    sems = pltpu.SemaphoreType.DMA((2, m))
    unit = 2 * rows * DH * half

    every, far, near = tuple(range(m)), (m - 1,), tuple(range(m - 1))

    def first_states(which):
        return call(
            partial(first_state_kernel, part, m, which),
            tuple(pltpu.with_memory_space_constraint(x, pltpu.HBM) for x in (keys, values)), [HBM, HBM],
            [state] * len(which), unit * len(which) // m, 6 * rows * half * len(which) // m, [slim, slim, sems],
        )

    def states_of(c):
        return call(
            partial(state_kernel, c, part, m), (keys, values), [VMEM, VMEM],
            [state] * m, unit, 4 * rows * half,
        )

    def local_of(c, args):
        return call(
            partial(local_kernel, c * half // DH), (*args, gain2), [VMEM] * 5,
            [wide, wide], 4 * unit, 12 * rows * half,
        )

    parts_a = first_states(every[::-1])[::-1]
    parts_a, queries, keys, values, cotangent = barrier((parts_a, queries, keys, values, cotangent))
    base = (queries, keys, values, cotangent)
    prefix, made = scan_chunks(
        parts_a, lambda: (states_of(1), base), n, True,
        lambda e: local_of(0, e), lambda e: local_of(1, e),
    )

    def attend(c, which, loc, sums, finish):
        return call(
            partial(attend_kernel, c, part, m, which, width if finish else 0),
            (queries, loc, made[c][0], *(prefix[c][j] for j in which), *sums),
            [VMEM] * (3 + len(which) + len(sums)), [wide, stat, stat],
            unit * len(which) // m, 4 * rows * half * len(which) // m, alias={1: 0},
        )

    att_a, *sums = attend(0, every, made[0][1], (), False)
    att_b = made[1][1]
    if m > 1:
        att_b, *sums = attend(1, near, att_b, sums, False)
    att_b, *scale = attend(1, far, att_b, sums, True)
    attended = (att_a, att_b)

    def grads_of(c, which, g):
        k = len(which)
        g, *parts = call(
            partial(grad_kernel, c, part, m, which), (queries, attended[c], made[c][0], *scale, *g),
            [VMEM] * (5 + len(g)), [slim] + [state] * k,
            unit * k // m, 4 * rows * half * k // m, alias={5: 0} if g else {},
        )
        return parts, g

    def back_local_of(c, g):
        return call(
            partial(back_local_kernel, c * half // DH), (queries, keys, values, g), [VMEM] * 4,
            [wide, wide], 8 * unit, 8 * rows * half,
        )

    parts_a, near_a = grads_of(0, far, ())
    if m > 1:
        parts, near_a = grads_of(0, near, (near_a,))
        parts_a = parts + parts_a

    def second_grads():
        parts_b, near_b = grads_of(1, every, ())
        return parts_b, (near_a, near_b)

    suffix, made = scan_chunks(
        parts_a, second_grads, n, False,
        lambda e: back_local_of(0, e[0]), lambda e: back_local_of(1, e[1]),
    )

    outs = ()
    for c, which in ((0, every), (1, every)):
        if not which:
            continue
        k = len(which)
        base = 4 + k
        outs = call(
            partial(finish_kernel, c, part, m, which),
            (keys, values, *made[c], *(suffix[c][j] for j in which), *outs),
            [VMEM] * (4 + k) + [HBM] * len(outs),
            [jax.ShapeDtypeStruct((rows, width), BF16)] * 2, 2 * unit * k // m, 8 * rows * half * k // m,
            [slim, slim, sems], out_specs=[HBM, HBM], alias={base: 0, base + 1: 1} if outs else {},
        )
    return tuple(outs)


def solution(mesh):
    spec = P(("dp", "seq"), None)
    return jax.shard_map(
        partial(shards, mesh.shape["seq"]),
        mesh=mesh,
        in_specs=(spec, spec, spec, P(), spec),
        out_specs=(spec, spec),
        check_vma=False,
    )
```

```python
from functools import partial

import jax
import jax.numpy as jnp
from jax import lax
from jax.experimental import pallas as pl
from jax.experimental.pallas import tpu as pltpu
from jax.sharding import PartitionSpec as P

DH = 128
EPS = 1e-05
CHUNKS = 2
F32 = jnp.float32
BF16 = jnp.bfloat16
NT = (((1,), (1,)), ((), ()))
NN = (((1,), (0,)), ((), ()))
TN = (((0,), (0,)), ((), ()))
VMEM = pl.BlockSpec(memory_space=pltpu.VMEM)
HBM = pl.BlockSpec(memory_space=pltpu.HBM)
barrier = lax.optimization_barrier


def mm(a, b, dims):
    return lax.dot_general(a, b, dims, preferred_element_type=F32)


def head(h):
    return slice(h * DH, (h + 1) * DH)


def head_at(offset, h):
    return pl.ds(pl.multiple_of(offset + h * DH, DH), DH)


def owned(member, j, part):
    return pl.multiple_of((member ^ j) * part, part)


def mask_of(t, later):
    rows = lax.broadcasted_iota(jnp.int32, (t, t), 0)
    cols = lax.broadcasted_iota(jnp.int32, (t, t), 1)
    return rows <= cols if later else rows >= cols


def first_state_kernel(part, m, which, k_hbm, v_hbm, *rest):
    outs, (k_ref, v_ref, sem) = rest[:-3], rest[-3:]
    member = lax.rem(lax.axis_index("seq"), m)
    copies = []
    for j in which:
        at = owned(member, j, part)
        pair = []
        for i, (src, dst) in enumerate(((k_hbm, k_ref), (v_hbm, v_ref))):
            here = pl.ds(at, part)
            copy = pltpu.make_async_copy(src.at[:, here], dst.at[:, here], sem.at[i, j])
            copy.start()
            pair.append(copy)
        copies.append((j, at, pair))
    for out, (j, at, pair) in zip(outs, copies):
        for copy in pair:
            copy.wait()
        for h in range(part // DH):
            a, b = k_ref[:, head_at(at, h)], v_ref[:, head_at(at, h)]
            out[head(h), :] = mm(a, b, TN).astype(BF16)


def state_kernel(chunk, part, m, which, k_ref, v_ref, *outs):
    member = lax.rem(lax.axis_index("seq"), m)
    for out, j in zip(outs, which):
        far = pl.multiple_of(chunk * m * part + owned(member, j, part), part)
        for h in range(part // DH):
            a, b = k_ref[:, head_at(far, h)], v_ref[:, head_at(far, h)]
            out[head(h), :] = mm(a, b, TN).astype(BF16)


def local_kernel(first, q_ref, k_ref, v_ref, c_ref, gain_ref, u_ref, loc_ref):
    mask = mask_of(q_ref.shape[0], False)
    for h in range(u_ref.shape[1] // DH):
        far = head(first + h)
        scores = mm(q_ref[:, far], k_ref[:, far], NT)
        weights = jnp.where(mask, scores, 0.0).astype(BF16)
        loc_ref[:, head(h)] = mm(weights, v_ref[:, far], NN)
        u_ref[:, head(h)] = c_ref[:, far].astype(F32) * gain_ref[:, far]


def attend_kernel(chunk, part, m, which, width, q_ref, loc_ref, u_ref, *rest):
    count = len(which)
    prefixes, before, (att_ref, ss_ref, su_ref) = rest[:count], rest[count:-3], rest[-3:]
    member = lax.rem(lax.axis_index("seq"), m)
    if before:
        ss, su = before[0][...], before[1][...]
    else:
        ss = jnp.zeros(ss_ref.shape, F32)
        su = jnp.zeros(su_ref.shape, F32)
    for pre, j in zip(prefixes, which):
        at = owned(member, j, part)
        for h in range(part // DH):
            here = head_at(at, h)
            far = head_at(chunk * m * part + at, h)
            att = loc_ref[:, here] + mm(q_ref[:, far], pre[head(h), :], NN)
            att_ref[:, here] = att
            ss = ss + att * att
            su = su + att * u_ref[:, here]
    if width:
        r = lax.rsqrt(jnp.sum(ss, axis=1, keepdims=True) / width + EPS)
        su = r * r * r * (jnp.sum(su, axis=1, keepdims=True) / width)
        ss = r
    ss_ref[...] = jnp.broadcast_to(ss, ss_ref.shape)
    su_ref[...] = jnp.broadcast_to(su, su_ref.shape)


def grad_kernel(chunk, part, m, which, q_ref, att_ref, u_ref, r_ref, s_ref, *rest):
    g_ref, outs = rest[-len(which) - 1], rest[-len(which) :]
    member = lax.rem(lax.axis_index("seq"), m)
    r = r_ref[...]
    s = s_ref[...]
    for out, j in zip(outs, which):
        at = owned(member, j, part)
        for h in range(part // DH):
            here = head_at(at, h)
            g = (u_ref[:, here] * r - att_ref[:, here] * s).astype(BF16)
            g_ref[:, here] = g
            far = head_at(chunk * m * part + at, h)
            out[head(h), :] = mm(q_ref[:, far], g, TN).astype(BF16)


def back_local_kernel(first, q_ref, k_ref, v_ref, g_ref, kl_ref, vl_ref):
    mask = mask_of(q_ref.shape[0], True)
    for h in range(g_ref.shape[1] // DH):
        q, k, v = (ref[:, head(first + h)] for ref in (q_ref, k_ref, v_ref))
        g = g_ref[:, head(h)]
        vw = jnp.where(mask, mm(v, g, NT), 0.0).astype(BF16)
        kl_ref[:, head(h)] = mm(vw, q, NN)
        kw = jnp.where(mask, mm(k, q, NT), 0.0).astype(BF16)
        vl_ref[:, head(h)] = mm(kw, g, NN)


def finish_kernel(chunk, part, m, which, k_ref, v_ref, kl_ref, vl_ref, *rest):
    suffixes = rest[: len(which)]
    kg_hbm, vg_hbm, kg_ref, vg_ref, sem = rest[-5:]
    member = lax.rem(lax.axis_index("seq"), m)
    copies = []
    for suf, j in zip(suffixes, which):
        at = owned(member, j, part)
        far = pl.multiple_of(chunk * m * part + at, part)
        for h in range(part // DH):
            here = head_at(at, h)
            s = suf[head(h), :]
            own = head_at(far, h)
            kg_ref[:, here] = (kl_ref[:, here] + mm(v_ref[:, own], s, NT)).astype(BF16)
            vg_ref[:, here] = (vl_ref[:, here] + mm(k_ref[:, own], s, NN)).astype(BF16)
        for i, (src, dst) in enumerate(((kg_ref, kg_hbm), (vg_ref, vg_hbm))):
            copy = pltpu.make_async_copy(src.at[:, pl.ds(at, part)], dst.at[:, pl.ds(far, part)], sem.at[i, j])
            copy.start()
            copies.append(copy)
    for copy in copies:
        copy.wait()


def total_kernel(*refs):
    acc = refs[0][...].astype(F32)
    for ref in refs[1:-1]:
        acc = acc + ref[...].astype(F32)
    refs[-1][...] = acc.astype(refs[-1].dtype)


def give_back_kernel(m, forward, groups, carry, *refs):
    group = lax.axis_index("seq") // m
    use = group > 0 if forward else group < groups - 1
    got, back = refs[:m], refs[m:]
    member = lax.rem(lax.axis_index("seq"), m)
    for j in range(m):
        acc = jnp.where(use, carry[...].astype(F32), 0.0)
        for i in range(m):
            if i != j:
                source, target = member ^ i, member ^ j
                take = (source < target) if forward else (source > target)
                acc = acc + jnp.where(take, got[i][...].astype(F32), 0.0)
        back[j][...] = acc.astype(BF16)


def call(kernel, args, in_specs, out_shape, flops, nbytes, scratch=(), out_specs=None, alias={}):
    return pl.pallas_call(
        kernel,
        in_specs=in_specs,
        out_specs=out_specs or [VMEM] * len(out_shape),
        out_shape=out_shape,
        scratch_shapes=scratch,
        input_output_aliases=alias,
        compiler_params=pltpu.CompilerParams(vmem_limit_bytes=8 << 20),
        cost_estimate=pl.CostEstimate(flops=flops // 4, bytes_accessed=nbytes // 4, transcendentals=0),
    )(*args)


def total_of(got, n):
    m = len(got)
    wire = BF16 if n // m == 2 else F32
    (total,) = call(total_kernel, got, [VMEM] * m, [pltpu.VMEM(got[0].shape, wire)], got[0].size, got[0].size)
    return total


def give_back(got, carry, n, forward):
    m = len(got)
    return call(
        partial(give_back_kernel, m, forward, n // m), (carry, *got), [VMEM] * (m + 1),
        [pltpu.VMEM(got[0].shape, BF16)] * m, got[0].size, got[0].size,
    )


def exchange(parts, n):
    m = len(parts)
    out = [parts[0]] + [None] * (m - 1)
    for j in range(m - 1, 0, -1):
        perm = [(i, (i // m) * m + ((i % m) ^ j)) for i in range(n)]
        out[j] = lax.ppermute(parts[j], "seq", perm)
    return out


def carry_groups(total, n, m, forward):
    groups = n // m
    group = lax.axis_index("seq") // m

    def shift(x, by):
        step = by * m if forward else n - by * m
        return lax.ppermute(x, "seq", [(i, (i + step) % n) for i in range(n)])

    def shift_in(x, by):
        inside = group >= by if forward else group < groups - by
        return jnp.where(inside, shift(x, by), 0.0)

    if groups == 1:
        return total
    if groups == 2:
        return shift(total, 1)
    run = shift_in(total, 1)
    by = 1
    while by < groups - 1:
        run = run + shift_in(run, by)
        by *= 2
    return run


def scan_chunks(first, second_of, n, forward, fill_a, fill_b):
    m = len(first)
    got_a = exchange(first, n)
    own, second, extra = second_of()
    got_a = [*own, *got_a[len(own) :]]
    got_b = exchange(second, n)
    if forward:
        made_a = fill_a(extra)
        made_b = fill_b(extra)
        got_b, made_a, made_b = barrier((got_b, made_a, made_b))
    else:
        got_a, extra = barrier((got_a, extra))
        made_a = fill_a(extra)
        got_b, made_a, extra = barrier((got_b, made_a, extra))
    carry_a = carry_groups(total_of(got_a, n), n, m, forward)
    carry_b = carry_groups(total_of(got_b, n), n, m, forward)
    if not forward:
        made_b = fill_b(extra)
    back_a = exchange(give_back(got_a, carry_a, n, forward), n)
    back_b = exchange(give_back(got_b, carry_b, n, forward), n)
    return (back_a, back_b), (made_a, made_b)


def shards(n, queries, keys, values, gain, cotangent):
    rows, width = queries.shape
    m = 4 if n % 4 == 0 else (2 if n % 2 == 0 else 1)
    half = width // CHUNKS
    part = half // m
    gain2 = gain.reshape(1, width)
    wide = pltpu.VMEM((rows, half), F32)
    slim = pltpu.VMEM((rows, half), BF16)
    stat = pltpu.VMEM((rows, DH), F32)
    state = pltpu.VMEM((part, DH), BF16)
    sems = pltpu.SemaphoreType.DMA((2, m))
    unit = 2 * rows * DH * half

    every, far, near = tuple(range(m)), (m - 1,), tuple(range(m - 1))
    away, own = (every[:0:-1], (0,)) if m > 1 else (every, ())

    def first_states(which):
        return call(
            partial(first_state_kernel, part, m, which),
            tuple(pltpu.with_memory_space_constraint(x, pltpu.HBM) for x in (keys, values)), [HBM, HBM],
            [state] * len(which), unit * len(which) // m, 6 * rows * half * len(which) // m, [slim, slim, sems],
        )

    def states_of(c, which):
        k = len(which)
        return call(
            partial(state_kernel, c, part, m, which), (keys, values), [VMEM, VMEM],
            [state] * k, unit * k // m, 4 * rows * half * k // m,
        )

    def local_of(c, args):
        return call(
            partial(local_kernel, c * half // DH), (*args, gain2), [VMEM] * 5,
            [wide, wide], 4 * unit, 12 * rows * half,
        )

    parts_a = first_states(away)[::-1]
    parts_a, queries, keys, values, cotangent = barrier((parts_a, queries, keys, values, cotangent))

    def first_others():
        return states_of(0, own) if own else [], states_of(1, every), (queries, keys, values, cotangent)

    prefix, made = scan_chunks(
        [None] * len(own) + list(parts_a), first_others, n, True,
        lambda e: local_of(0, e), lambda e: local_of(1, e),
    )

    def attend(c, which, loc, sums, finish):
        return call(
            partial(attend_kernel, c, part, m, which, width if finish else 0),
            (queries, loc, made[c][0], *(prefix[c][j] for j in which), *sums),
            [VMEM] * (3 + len(which) + len(sums)), [wide, stat, stat],
            unit * len(which) // m, 4 * rows * half * len(which) // m, alias={1: 0},
        )

    att_a, *sums = attend(0, every, made[0][1], (), False)
    att_b = made[1][1]
    if m > 1:
        att_b, *sums = attend(1, near, att_b, sums, False)
    att_b, *scale = attend(1, far, att_b, sums, True)
    attended = (att_a, att_b)

    def grads_of(c, which, g):
        k = len(which)
        g, *parts = call(
            partial(grad_kernel, c, part, m, which), (queries, attended[c], made[c][0], *scale, *g),
            [VMEM] * (5 + len(g)), [slim] + [state] * k,
            unit * k // m, 4 * rows * half * k // m, alias={5: 0} if g else {},
        )
        return parts, g

    def back_local_of(c, g):
        return call(
            partial(back_local_kernel, c * half // DH), (queries, keys, values, g), [VMEM] * 4,
            [wide, wide], 8 * unit, 8 * rows * half,
        )

    parts_a, near_a = grads_of(0, away, ())

    def second_grads():
        mine, g_a = grads_of(0, own, (near_a,)) if own else ([], near_a)
        parts_b, g_b = grads_of(1, every, ())
        return mine, parts_b, (g_a, g_b)

    suffix, made = scan_chunks(
        [None] * len(own) + parts_a[::-1], second_grads, n, False,
        lambda e: back_local_of(0, e[0]), lambda e: back_local_of(1, e[1]),
    )

    outs = ()
    for c, which in ((0, every), (1, every)):
        if not which:
            continue
        k = len(which)
        base = 4 + k
        outs = call(
            partial(finish_kernel, c, part, m, which),
            (keys, values, *made[c], *(suffix[c][j] for j in which), *outs),
            [VMEM] * (4 + k) + [HBM] * len(outs),
            [jax.ShapeDtypeStruct((rows, width), BF16)] * 2, 2 * unit * k // m, 8 * rows * half * k // m,
            [slim, slim, sems], out_specs=[HBM, HBM], alias={base: 0, base + 1: 1} if outs else {},
        )
    return tuple(outs)


def solution(mesh):
    spec = P(("dp", "seq"), None)
    return jax.shard_map(
        partial(shards, mesh.shape["seq"]),
        mesh=mesh,
        in_specs=(spec, spec, spec, P(), spec),
        out_specs=(spec, spec),
        check_vma=False,
    )
```

```python
from functools import partial

import jax
import jax.numpy as jnp
from jax import lax
from jax.experimental import pallas as pl
from jax.experimental.pallas import tpu as pltpu
from jax.sharding import PartitionSpec as P

DH = 128
EPS = 1e-05
CHUNKS = 2
F32 = jnp.float32
BF16 = jnp.bfloat16
NT = (((1,), (1,)), ((), ()))
NN = (((1,), (0,)), ((), ()))
TN = (((0,), (0,)), ((), ()))
VMEM = pl.BlockSpec(memory_space=pltpu.VMEM)
HBM = pl.BlockSpec(memory_space=pltpu.HBM)
barrier = lax.optimization_barrier


def mm(a, b, dims):
    return lax.dot_general(a, b, dims, preferred_element_type=F32)


def head(h):
    return slice(h * DH, (h + 1) * DH)


def head_at(offset, h):
    return pl.ds(pl.multiple_of(offset + h * DH, DH), DH)


def owned(member, j, part):
    return pl.multiple_of((member ^ j) * part, part)


def mask_of(t, later):
    rows = lax.broadcasted_iota(jnp.int32, (t, t), 0)
    cols = lax.broadcasted_iota(jnp.int32, (t, t), 1)
    return rows <= cols if later else rows >= cols


def first_state_kernel(part, m, which, k_hbm, v_hbm, *rest):
    outs, (k_ref, v_ref, sem) = rest[:-3], rest[-3:]
    member = lax.rem(lax.axis_index("seq"), m)
    copies = []
    for j in which:
        at = owned(member, j, part)
        pair = []
        for i, (src, dst) in enumerate(((k_hbm, k_ref), (v_hbm, v_ref))):
            here = pl.ds(at, part)
            copy = pltpu.make_async_copy(src.at[:, here], dst.at[:, here], sem.at[i, j])
            copy.start()
            pair.append(copy)
        copies.append((j, at, pair))
    for out, (j, at, pair) in zip(outs, copies):
        for copy in pair:
            copy.wait()
        for h in range(part // DH):
            a, b = k_ref[:, head_at(at, h)], v_ref[:, head_at(at, h)]
            out[head(h), :] = mm(a, b, TN).astype(BF16)


def state_kernel(chunk, part, m, which, k_ref, v_ref, *outs):
    member = lax.rem(lax.axis_index("seq"), m)
    for out, j in zip(outs, which):
        far = pl.multiple_of(chunk * m * part + owned(member, j, part), part)
        for h in range(part // DH):
            a, b = k_ref[:, head_at(far, h)], v_ref[:, head_at(far, h)]
            out[head(h), :] = mm(a, b, TN).astype(BF16)


def local_kernel(first, q_ref, k_ref, v_ref, c_ref, gain_ref, u_ref, loc_ref):
    mask = mask_of(q_ref.shape[0], False)
    for h in range(u_ref.shape[1] // DH):
        far = head(first + h)
        scores = mm(q_ref[:, far], k_ref[:, far], NT)
        weights = jnp.where(mask, scores, 0.0).astype(BF16)
        loc_ref[:, head(h)] = mm(weights, v_ref[:, far], NN)
        u_ref[:, head(h)] = c_ref[:, far].astype(F32) * gain_ref[:, far]


def attend_kernel(chunk, part, m, which, width, q_ref, loc_ref, u_ref, *rest):
    count = len(which)
    prefixes, before, (att_ref, ss_ref, su_ref) = rest[:count], rest[count:-3], rest[-3:]
    member = lax.rem(lax.axis_index("seq"), m)
    if before:
        ss, su = before[0][...], before[1][...]
    else:
        ss = jnp.zeros(ss_ref.shape, F32)
        su = jnp.zeros(su_ref.shape, F32)
    for pre, j in zip(prefixes, which):
        at = owned(member, j, part)
        for h in range(part // DH):
            here = head_at(at, h)
            far = head_at(chunk * m * part + at, h)
            att = loc_ref[:, here] + mm(q_ref[:, far], pre[head(h), :], NN)
            att_ref[:, here] = att
            ss = ss + att * att
            su = su + att * u_ref[:, here]
    if width:
        r = lax.rsqrt(jnp.sum(ss, axis=1, keepdims=True) / width + EPS)
        su = r * r * r * (jnp.sum(su, axis=1, keepdims=True) / width)
        ss = r
    ss_ref[...] = jnp.broadcast_to(ss, ss_ref.shape)
    su_ref[...] = jnp.broadcast_to(su, su_ref.shape)


def grad_kernel(chunk, part, m, which, q_ref, att_ref, u_ref, r_ref, s_ref, *rest):
    g_ref, outs = rest[-len(which) - 1], rest[-len(which) :]
    member = lax.rem(lax.axis_index("seq"), m)
    r = r_ref[...]
    s = s_ref[...]
    for out, j in zip(outs, which):
        at = owned(member, j, part)
        for h in range(part // DH):
            here = head_at(at, h)
            g = (u_ref[:, here] * r - att_ref[:, here] * s).astype(BF16)
            g_ref[:, here] = g
            far = head_at(chunk * m * part + at, h)
            out[head(h), :] = mm(q_ref[:, far], g, TN).astype(BF16)


def back_local_kernel(first, q_ref, k_ref, v_ref, g_ref, kl_ref, vl_ref):
    mask = mask_of(q_ref.shape[0], True)
    for h in range(g_ref.shape[1] // DH):
        q, k, v = (ref[:, head(first + h)] for ref in (q_ref, k_ref, v_ref))
        g = g_ref[:, head(h)]
        vw = jnp.where(mask, mm(v, g, NT), 0.0).astype(BF16)
        kl_ref[:, head(h)] = mm(vw, q, NN)
        kw = jnp.where(mask, mm(k, q, NT), 0.0).astype(BF16)
        vl_ref[:, head(h)] = mm(kw, g, NN)


def finish_kernel(chunk, part, m, which, k_ref, v_ref, kl_ref, vl_ref, *rest):
    suffixes = rest[: len(which)]
    kg_hbm, vg_hbm, kg_ref, vg_ref, sem = rest[-5:]
    member = lax.rem(lax.axis_index("seq"), m)
    copies = []
    for suf, j in zip(suffixes, which):
        at = owned(member, j, part)
        far = pl.multiple_of(chunk * m * part + at, part)
        for h in range(part // DH):
            here = head_at(at, h)
            s = suf[head(h), :]
            own = head_at(far, h)
            kg_ref[:, here] = (kl_ref[:, here] + mm(v_ref[:, own], s, NT)).astype(BF16)
            vg_ref[:, here] = (vl_ref[:, here] + mm(k_ref[:, own], s, NN)).astype(BF16)
        for i, (src, dst) in enumerate(((kg_ref, kg_hbm), (vg_ref, vg_hbm))):
            copy = pltpu.make_async_copy(src.at[:, pl.ds(at, part)], dst.at[:, pl.ds(far, part)], sem.at[i, j])
            copy.start()
            copies.append(copy)
    for copy in copies:
        copy.wait()


def total_kernel(*refs):
    acc = refs[0][...].astype(F32)
    for ref in refs[1:-1]:
        acc = acc + ref[...].astype(F32)
    refs[-1][...] = acc.astype(refs[-1].dtype)


def give_back_kernel(m, forward, groups, carry, *refs):
    group = lax.axis_index("seq") // m
    use = group > 0 if forward else group < groups - 1
    got, back = refs[:m], refs[m:]
    member = lax.rem(lax.axis_index("seq"), m)
    for j in range(m):
        acc = jnp.where(use, carry[...].astype(F32), 0.0)
        for i in range(m):
            if i != j:
                source, target = member ^ i, member ^ j
                take = (source < target) if forward else (source > target)
                acc = acc + jnp.where(take, got[i][...].astype(F32), 0.0)
        back[j][...] = acc.astype(BF16)


def call(kernel, args, in_specs, out_shape, flops, nbytes, scratch=(), out_specs=None, alias={}):
    return pl.pallas_call(
        kernel,
        in_specs=in_specs,
        out_specs=out_specs or [VMEM] * len(out_shape),
        out_shape=out_shape,
        scratch_shapes=scratch,
        input_output_aliases=alias,
        compiler_params=pltpu.CompilerParams(vmem_limit_bytes=8 << 20),
        cost_estimate=pl.CostEstimate(flops=flops, bytes_accessed=nbytes, transcendentals=0),
    )(*args)


def total_of(got, n):
    m = len(got)
    wire = BF16 if n // m == 2 else F32
    (total,) = call(total_kernel, got, [VMEM] * m, [pltpu.VMEM(got[0].shape, wire)], got[0].size, got[0].size)
    return total


def give_back(got, carry, n, forward):
    m = len(got)
    return call(
        partial(give_back_kernel, m, forward, n // m), (carry, *got), [VMEM] * (m + 1),
        [pltpu.VMEM(got[0].shape, BF16)] * m, got[0].size, got[0].size,
    )


def exchange(parts, n):
    m = len(parts)
    out = [parts[0]] + [None] * (m - 1)
    for j in range(m - 1, 0, -1):
        perm = [(i, (i // m) * m + ((i % m) ^ j)) for i in range(n)]
        out[j] = lax.ppermute(parts[j], "seq", perm)
    return out


def carry_groups(total, n, m, forward):
    groups = n // m
    group = lax.axis_index("seq") // m

    def shift(x, by):
        step = by * m if forward else n - by * m
        return lax.ppermute(x, "seq", [(i, (i + step) % n) for i in range(n)])

    def shift_in(x, by):
        inside = group >= by if forward else group < groups - by
        return jnp.where(inside, shift(x, by), 0.0)

    if groups == 1:
        return total
    if groups == 2:
        return shift(total, 1)
    run = shift_in(total, 1)
    by = 1
    while by < groups - 1:
        run = run + shift_in(run, by)
        by *= 2
    return run


def scan_chunks(first, second_of, n, forward, fill_a, fill_b):
    m = len(first)
    got_a = exchange(first, n)
    own, second, extra = second_of()
    got_a = [*own, *got_a[len(own) :]]
    got_b = exchange(second, n)
    if forward:
        made_b = fill_b(extra)
        got_b, made_b, extra = barrier((got_b, made_b, extra))
        made_a = fill_a(extra)
    else:
        got_a, extra = barrier((got_a, extra))
        made_a = fill_a(extra)
        got_b, made_a, extra = barrier((got_b, made_a, extra))
    carry_a = carry_groups(total_of(got_a, n), n, m, forward)
    carry_b = carry_groups(total_of(got_b, n), n, m, forward)
    if not forward:
        made_b = fill_b(extra)
    back_a = exchange(give_back(got_a, carry_a, n, forward), n)
    back_b = exchange(give_back(got_b, carry_b, n, forward), n)
    return (back_a, back_b), (made_a, made_b)


def shards(n, queries, keys, values, gain, cotangent):
    rows, width = queries.shape
    m = 4 if n % 4 == 0 else (2 if n % 2 == 0 else 1)
    half = width // CHUNKS
    part = half // m
    gain2 = gain.reshape(1, width)
    wide = pltpu.VMEM((rows, half), F32)
    slim = pltpu.VMEM((rows, half), BF16)
    stat = pltpu.VMEM((rows, DH), F32)
    state = pltpu.VMEM((part, DH), BF16)
    sems = pltpu.SemaphoreType.DMA((2, m))
    unit = 2 * rows * DH * half

    every, far, near = tuple(range(m)), (m - 1,), tuple(range(m - 1))
    away, own = (every[:0:-1], (0,)) if m > 1 else (every, ())

    def first_states(which):
        return call(
            partial(first_state_kernel, part, m, which),
            tuple(pltpu.with_memory_space_constraint(x, pltpu.HBM) for x in (keys, values)), [HBM, HBM],
            [state] * len(which), unit * len(which) // m, 6 * rows * half * len(which) // m, [slim, slim, sems],
        )

    def states_of(c, which):
        k = len(which)
        return call(
            partial(state_kernel, c, part, m, which), (keys, values), [VMEM, VMEM],
            [state] * k, unit * k // m, 4 * rows * half * k // m,
        )

    def local_of(c, args):
        return call(
            partial(local_kernel, c * half // DH), (*args, gain2), [VMEM] * 5,
            [wide, wide], 4 * unit, 12 * rows * half,
        )

    parts_a = first_states(away)[::-1]
    parts_a, queries, keys, values, cotangent = barrier((parts_a, queries, keys, values, cotangent))

    def first_others():
        return states_of(0, own) if own else [], states_of(1, every), (queries, keys, values, cotangent)

    prefix, made = scan_chunks(
        [None] * len(own) + list(parts_a), first_others, n, True,
        lambda e: local_of(0, e), lambda e: local_of(1, e),
    )

    def attend(c, which, loc, sums, finish):
        return call(
            partial(attend_kernel, c, part, m, which, width if finish else 0),
            (queries, loc, made[c][0], *(prefix[c][j] for j in which), *sums),
            [VMEM] * (3 + len(which) + len(sums)), [wide, stat, stat],
            unit * len(which) // m, 4 * rows * half * len(which) // m, alias={1: 0},
        )

    att_a, *sums = attend(0, every, made[0][1], (), False)
    att_b = made[1][1]
    if m > 1:
        att_b, *sums = attend(1, near, att_b, sums, False)
    att_b, *scale = attend(1, far, att_b, sums, True)
    attended = (att_a, att_b)

    def grads_of(c, which, g):
        k = len(which)
        g, *parts = call(
            partial(grad_kernel, c, part, m, which), (queries, attended[c], made[c][0], *scale, *g),
            [VMEM] * (5 + len(g)), [slim] + [state] * k,
            unit * k // m, 4 * rows * half * k // m, alias={5: 0} if g else {},
        )
        return parts, g

    def back_local_of(c, g):
        return call(
            partial(back_local_kernel, c * half // DH), (queries, keys, values, g), [VMEM] * 4,
            [wide, wide], 8 * unit, 8 * rows * half,
        )

    parts_a, near_a = grads_of(0, away, ())

    def second_grads():
        mine, g_a = grads_of(0, own, (near_a,)) if own else ([], near_a)
        parts_b, g_b = grads_of(1, every, ())
        return mine, parts_b, (g_a, g_b)

    suffix, made = scan_chunks(
        [None] * len(own) + parts_a[::-1], second_grads, n, False,
        lambda e: back_local_of(0, e[0]), lambda e: back_local_of(1, e[1]),
    )

    outs = ()
    for c, which in ((0, every), (1, every)):
        if not which:
            continue
        k = len(which)
        base = 4 + k
        outs = call(
            partial(finish_kernel, c, part, m, which),
            (keys, values, *made[c], *(suffix[c][j] for j in which), *outs),
            [VMEM] * (4 + k) + [HBM] * len(outs),
            [jax.ShapeDtypeStruct((rows, width), BF16)] * 2, 2 * unit * k // m, 8 * rows * half * k // m,
            [slim, slim, sems], out_specs=[HBM, HBM], alias={base: 0, base + 1: 1} if outs else {},
        )
    return tuple(outs)


def solution(mesh):
    spec = P(("dp", "seq"), None)
    return jax.shard_map(
        partial(shards, mesh.shape["seq"]),
        mesh=mesh,
        in_specs=(spec, spec, spec, P(), spec),
        out_specs=(spec, spec),
        check_vma=False,
    )
```

```python
from functools import partial

import jax
import jax.numpy as jnp
from jax import lax
from jax.experimental import pallas as pl
from jax.experimental.pallas import tpu as pltpu
from jax.sharding import PartitionSpec as P

DH = 128
EPS = 1e-05
CHUNKS = 2
F32 = jnp.float32
BF16 = jnp.bfloat16
NT = (((1,), (1,)), ((), ()))
NN = (((1,), (0,)), ((), ()))
TN = (((0,), (0,)), ((), ()))
VMEM = pl.BlockSpec(memory_space=pltpu.VMEM)
HBM = pl.BlockSpec(memory_space=pltpu.HBM)
barrier = lax.optimization_barrier


def mm(a, b, dims):
    return lax.dot_general(a, b, dims, preferred_element_type=F32)


def head(h):
    return slice(h * DH, (h + 1) * DH)


def head_at(offset, h):
    return pl.ds(pl.multiple_of(offset + h * DH, DH), DH)


def owned(member, j, part):
    return pl.multiple_of((member ^ j) * part, part)


def mask_of(t, later):
    rows = lax.broadcasted_iota(jnp.int32, (t, t), 0)
    cols = lax.broadcasted_iota(jnp.int32, (t, t), 1)
    return rows <= cols if later else rows >= cols


def first_state_kernel(part, m, which, k_hbm, v_hbm, *rest):
    outs, (k_ref, v_ref, sem) = rest[:-3], rest[-3:]
    member = lax.rem(lax.axis_index("seq"), m)
    copies = []
    for j in which:
        at = owned(member, j, part)
        pair = []
        for i, (src, dst) in enumerate(((k_hbm, k_ref), (v_hbm, v_ref))):
            here = pl.ds(at, part)
            copy = pltpu.make_async_copy(src.at[:, here], dst.at[:, here], sem.at[i, j])
            copy.start()
            pair.append(copy)
        copies.append((j, at, pair))
    for out, (j, at, pair) in zip(outs, copies):
        for copy in pair:
            copy.wait()
        for h in range(part // DH):
            a, b = k_ref[:, head_at(at, h)], v_ref[:, head_at(at, h)]
            out[head(h), :] = mm(a, b, TN).astype(BF16)


def state_kernel(chunk, part, m, which, k_ref, v_ref, *outs):
    member = lax.rem(lax.axis_index("seq"), m)
    for out, j in zip(outs, which):
        far = pl.multiple_of(chunk * m * part + owned(member, j, part), part)
        for h in range(part // DH):
            a, b = k_ref[:, head_at(far, h)], v_ref[:, head_at(far, h)]
            out[head(h), :] = mm(a, b, TN).astype(BF16)


def local_kernel(first, q_ref, k_ref, v_ref, c_ref, gain_ref, u_ref, loc_ref):
    mask = mask_of(q_ref.shape[0], False)
    for h in range(u_ref.shape[1] // DH):
        far = head(first + h)
        scores = mm(q_ref[:, far], k_ref[:, far], NT)
        weights = jnp.where(mask, scores, 0.0).astype(BF16)
        loc_ref[:, head(h)] = mm(weights, v_ref[:, far], NN)
        u_ref[:, head(h)] = c_ref[:, far].astype(F32) * gain_ref[:, far]


def attend_kernel(chunk, part, m, which, width, q_ref, loc_ref, u_ref, *rest):
    count = len(which)
    prefixes, before, (att_ref, ss_ref, su_ref) = rest[:count], rest[count:-3], rest[-3:]
    member = lax.rem(lax.axis_index("seq"), m)
    if before:
        ss, su = before[0][...], before[1][...]
    else:
        ss = jnp.zeros(ss_ref.shape, F32)
        su = jnp.zeros(su_ref.shape, F32)
    for pre, j in zip(prefixes, which):
        at = owned(member, j, part)
        for h in range(part // DH):
            here = head_at(at, h)
            far = head_at(chunk * m * part + at, h)
            att = loc_ref[:, here] + mm(q_ref[:, far], pre[head(h), :], NN)
            att_ref[:, here] = att
            ss = ss + att * att
            su = su + att * u_ref[:, here]
    if width:
        r = lax.rsqrt(jnp.sum(ss, axis=1, keepdims=True) / width + EPS)
        su = r * r * r * (jnp.sum(su, axis=1, keepdims=True) / width)
        ss = r
    ss_ref[...] = jnp.broadcast_to(ss, ss_ref.shape)
    su_ref[...] = jnp.broadcast_to(su, su_ref.shape)


def grad_kernel(chunk, part, m, which, q_ref, att_ref, u_ref, r_ref, s_ref, *rest):
    g_ref, outs = rest[-len(which) - 1], rest[-len(which) :]
    member = lax.rem(lax.axis_index("seq"), m)
    r = r_ref[...]
    s = s_ref[...]
    for out, j in zip(outs, which):
        at = owned(member, j, part)
        for h in range(part // DH):
            here = head_at(at, h)
            g = (u_ref[:, here] * r - att_ref[:, here] * s).astype(BF16)
            g_ref[:, here] = g
            far = head_at(chunk * m * part + at, h)
            out[head(h), :] = mm(q_ref[:, far], g, TN).astype(BF16)


def back_local_kernel(first, q_ref, k_ref, v_ref, g_ref, kl_ref, vl_ref):
    mask = mask_of(q_ref.shape[0], True)
    for h in range(g_ref.shape[1] // DH):
        q, k, v = (ref[:, head(first + h)] for ref in (q_ref, k_ref, v_ref))
        g = g_ref[:, head(h)]
        vw = jnp.where(mask, mm(v, g, NT), 0.0).astype(BF16)
        kl_ref[:, head(h)] = mm(vw, q, NN)
        kw = jnp.where(mask, mm(k, q, NT), 0.0).astype(BF16)
        vl_ref[:, head(h)] = mm(kw, g, NN)


def finish_kernel(chunk, part, m, which, k_ref, v_ref, kl_ref, vl_ref, *rest):
    suffixes = rest[: len(which)]
    kg_hbm, vg_hbm, kg_ref, vg_ref, sem = rest[-5:]
    member = lax.rem(lax.axis_index("seq"), m)
    copies = []
    for suf, j in zip(suffixes, which):
        at = owned(member, j, part)
        far = pl.multiple_of(chunk * m * part + at, part)
        for h in range(part // DH):
            here = head_at(at, h)
            s = suf[head(h), :]
            own = head_at(far, h)
            kg_ref[:, here] = (kl_ref[:, here] + mm(v_ref[:, own], s, NT)).astype(BF16)
            vg_ref[:, here] = (vl_ref[:, here] + mm(k_ref[:, own], s, NN)).astype(BF16)
        for i, (src, dst) in enumerate(((kg_ref, kg_hbm), (vg_ref, vg_hbm))):
            copy = pltpu.make_async_copy(src.at[:, pl.ds(at, part)], dst.at[:, pl.ds(far, part)], sem.at[i, j])
            copy.start()
            copies.append(copy)
    for copy in copies:
        copy.wait()


def total_kernel(*refs):
    acc = refs[0][...].astype(F32)
    for ref in refs[1:-1]:
        acc = acc + ref[...].astype(F32)
    refs[-1][...] = acc.astype(refs[-1].dtype)


def give_back_kernel(m, forward, groups, carry, *refs):
    group = lax.axis_index("seq") // m
    use = group > 0 if forward else group < groups - 1
    got, back = refs[:m], refs[m:]
    member = lax.rem(lax.axis_index("seq"), m)
    for j in range(m):
        acc = jnp.where(use, carry[...].astype(F32), 0.0)
        for i in range(m):
            if i != j:
                source, target = member ^ i, member ^ j
                take = (source < target) if forward else (source > target)
                acc = acc + jnp.where(take, got[i][...].astype(F32), 0.0)
        back[j][...] = acc.astype(BF16)


def call(kernel, args, in_specs, out_shape, flops, nbytes, scratch=(), out_specs=None, alias={}):
    return pl.pallas_call(
        kernel,
        in_specs=in_specs,
        out_specs=out_specs or [VMEM] * len(out_shape),
        out_shape=out_shape,
        scratch_shapes=scratch,
        input_output_aliases=alias,
        compiler_params=pltpu.CompilerParams(vmem_limit_bytes=8 << 20),
        cost_estimate=pl.CostEstimate(flops=flops // 4, bytes_accessed=nbytes // 4, transcendentals=0),
    )(*args)


def total_of(got, n):
    m = len(got)
    wire = BF16 if n // m == 2 else F32
    (total,) = call(total_kernel, got, [VMEM] * m, [pltpu.VMEM(got[0].shape, wire)], got[0].size, got[0].size)
    return total


def give_back(got, carry, n, forward):
    m = len(got)
    return call(
        partial(give_back_kernel, m, forward, n // m), (carry, *got), [VMEM] * (m + 1),
        [pltpu.VMEM(got[0].shape, BF16)] * m, got[0].size, got[0].size,
    )


def exchange(parts, n):
    m = len(parts)
    out = [parts[0]] + [None] * (m - 1)
    for j in range(m - 1, 0, -1):
        perm = [(i, (i // m) * m + ((i % m) ^ j)) for i in range(n)]
        out[j] = lax.ppermute(parts[j], "seq", perm)
    return out


def carry_groups(total, n, m, forward):
    groups = n // m
    group = lax.axis_index("seq") // m

    def shift(x, by):
        step = by * m if forward else n - by * m
        return lax.ppermute(x, "seq", [(i, (i + step) % n) for i in range(n)])

    def shift_in(x, by):
        inside = group >= by if forward else group < groups - by
        return jnp.where(inside, shift(x, by), 0.0)

    if groups == 1:
        return total
    if groups == 2:
        return shift(total, 1)
    run = shift_in(total, 1)
    by = 1
    while by < groups - 1:
        run = run + shift_in(run, by)
        by *= 2
    return run


def scan_chunks(first, second_of, n, forward, fill_a, fill_b):
    m = len(first)
    got_a = exchange(first, n)
    own, second, extra = second_of()
    got_a = [*own, *got_a[len(own) :]]
    got_b = exchange(second, n)
    if forward:
        made_b = fill_b(extra)
        got_b, made_b, extra = barrier((got_b, made_b, extra))
        made_a = fill_a(extra)
    else:
        got_a, extra = barrier((got_a, extra))
        made_a = fill_a(extra)
        got_b, made_a, extra = barrier((got_b, made_a, extra))
    carry_a = carry_groups(total_of(got_a, n), n, m, forward)
    carry_b = carry_groups(total_of(got_b, n), n, m, forward)
    if not forward:
        back = give_back(got_a, carry_a, n, forward)
        back, extra = barrier((back, extra))
        made_b = fill_b(extra)
        back_a = exchange(back, n)
    else:
        back_a = exchange(give_back(got_a, carry_a, n, forward), n)
    back_b = exchange(give_back(got_b, carry_b, n, forward), n)
    return (back_a, back_b), (made_a, made_b)


def shards(n, queries, keys, values, gain, cotangent):
    rows, width = queries.shape
    m = 4 if n % 4 == 0 else (2 if n % 2 == 0 else 1)
    half = width // CHUNKS
    part = half // m
    gain2 = gain.reshape(1, width)
    wide = pltpu.VMEM((rows, half), F32)
    slim = pltpu.VMEM((rows, half), BF16)
    stat = pltpu.VMEM((rows, DH), F32)
    state = pltpu.VMEM((part, DH), BF16)
    sems = pltpu.SemaphoreType.DMA((2, m))
    unit = 2 * rows * DH * half

    every, far, near = tuple(range(m)), (m - 1,), tuple(range(m - 1))
    away, own = (every[:0:-1], (0,)) if m > 1 else (every, ())

    def first_states(which):
        return call(
            partial(first_state_kernel, part, m, which),
            tuple(pltpu.with_memory_space_constraint(x, pltpu.HBM) for x in (keys, values)), [HBM, HBM],
            [state] * len(which), unit * len(which) // m, 6 * rows * half * len(which) // m, [slim, slim, sems],
        )

    def states_of(c, which):
        k = len(which)
        return call(
            partial(state_kernel, c, part, m, which), (keys, values), [VMEM, VMEM],
            [state] * k, unit * k // m, 4 * rows * half * k // m,
        )

    def local_of(c, args):
        return call(
            partial(local_kernel, c * half // DH), (*args, gain2), [VMEM] * 5,
            [wide, wide], 4 * unit, 12 * rows * half,
        )

    parts_a = first_states(away)[::-1]
    parts_a, queries, keys, values, cotangent = barrier((parts_a, queries, keys, values, cotangent))

    def first_others():
        return states_of(0, own) if own else [], states_of(1, every), (queries, keys, values, cotangent)

    prefix, made = scan_chunks(
        [None] * len(own) + list(parts_a), first_others, n, True,
        lambda e: local_of(0, e), lambda e: local_of(1, e),
    )

    def attend(c, which, loc, sums, finish):
        return call(
            partial(attend_kernel, c, part, m, which, width if finish else 0),
            (queries, loc, made[c][0], *(prefix[c][j] for j in which), *sums),
            [VMEM] * (3 + len(which) + len(sums)), [wide, stat, stat],
            unit * len(which) // m, 4 * rows * half * len(which) // m, alias={1: 0},
        )

    att_a, *sums = attend(0, every, made[0][1], (), False)
    att_b = made[1][1]
    if m > 1:
        att_b, *sums = attend(1, near, att_b, sums, False)
    att_b, *scale = attend(1, far, att_b, sums, True)
    attended = (att_a, att_b)

    def grads_of(c, which, g):
        k = len(which)
        g, *parts = call(
            partial(grad_kernel, c, part, m, which), (queries, attended[c], made[c][0], *scale, *g),
            [VMEM] * (5 + len(g)), [slim] + [state] * k,
            unit * k // m, 4 * rows * half * k // m, alias={5: 0} if g else {},
        )
        return parts, g

    def back_local_of(c, g):
        return call(
            partial(back_local_kernel, c * half // DH), (queries, keys, values, g), [VMEM] * 4,
            [wide, wide], 8 * unit, 8 * rows * half,
        )

    parts_a, near_a = grads_of(0, away, ())

    def second_grads():
        mine, g_a = grads_of(0, own, (near_a,)) if own else ([], near_a)
        parts_b, g_b = grads_of(1, every, ())
        return mine, parts_b, (g_a, g_b)

    suffix, made = scan_chunks(
        [None] * len(own) + parts_a[::-1], second_grads, n, False,
        lambda e: back_local_of(0, e[0]), lambda e: back_local_of(1, e[1]),
    )

    outs = ()
    for c, which in ((0, every), (1, every)):
        if not which:
            continue
        k = len(which)
        base = 4 + k
        outs = call(
            partial(finish_kernel, c, part, m, which),
            (keys, values, *made[c], *(suffix[c][j] for j in which), *outs),
            [VMEM] * (4 + k) + [HBM] * len(outs),
            [jax.ShapeDtypeStruct((rows, width), BF16)] * 2, 2 * unit * k // m, 8 * rows * half * k // m,
            [slim, slim, sems], out_specs=[HBM, HBM], alias={base: 0, base + 1: 1} if outs else {},
        )
    return tuple(outs)


def solution(mesh):
    spec = P(("dp", "seq"), None)
    return jax.shard_map(
        partial(shards, mesh.shape["seq"]),
        mesh=mesh,
        in_specs=(spec, spec, spec, P(), spec),
        out_specs=(spec, spec),
        check_vma=False,
    )
```
